32 devices in a mesh: grp: 2 (over x), seq: 8 (over z, y), dp: 2 (over core).
Axes of the slice: x: 2, y: 2, z: 4, core: 2. Of those that a mesh axis runs over, the one named last changes fastest.
Arguments:
- dec_query: bfloat16 [4, 1024, 2048], P(('grp', 'dp'), 'seq'), parts along dimension 0, may hold values from -9 to 9
- enc_key: bfloat16 [4, 4096, 2048], P(('grp', 'dp'), 'seq'), parts along dimension 0, may hold values from -4 to 4
- enc_value: bfloat16 [4, 4096, 2048], P(('grp', 'dp'), 'seq'), parts along dimension 0, may hold values from -6 to 6
- saved_out: bfloat16 [4, 1024, 2048], P(('grp', 'dp'), 'seq'), parts along dimension 0, may hold values from -3 to 3
- d_out: bfloat16 [4, 1024, 2048], P(('grp', 'dp'), 'seq'), parts along dimension 0, may hold values from -24 to 24
- dec_start: int32 [4, 33], P(('grp', 'dp')), parts along dimension 0, may hold values from 0 to 1024, as said below
- enc_start: int32 [4, 33], P(('grp', 'dp')), parts along dimension 0, may hold values from 0 to 4096, as said below
Outputs:
- d_query: bfloat16 [4, 1024, 2048], P(('grp', 'dp'), 'seq'), parts along dimension 0
- d_key: bfloat16 [4, 4096, 2048], P(('grp', 'dp'), 'seq'), parts along dimension 0
- d_value: bfloat16 [4, 4096, 2048], P(('grp', 'dp'), 'seq'), parts along dimension 0
The draws below stay inside these ranges and needn't reach their ends.
There are 2 independent parts, one for each index of `grp`. The reference program is written for one: setup_inputs(seed, part) draws one part's arguments, and reference() takes and returns one part's arrays. A program takes and returns all parts, laid end to end along the dimension named above; each array names one. Nothing has to cross between parts.
Inputs may be any that keep to these rules, and one draw needn't show every extreme that they name: dec_start[b, 0] = 0 and dec_start[b, 32] = 1024; dec_start[b, k] = k * 32 plus a whole number from 0 to 16, so an example has 16 to 48 decoder tokens, and in every batch one example has exactly 48. enc_start[b, 0] = 0 and enc_start[b, 32] = 4096; enc_start[b, k] = k * 4 * 32 plus a whole number from 0 to 64, so an example has 64 to 192 encoder tokens, and in every batch one example has exactly 192.
All inputs are finite; a program needn't handle non-finite values.
Results may differ from the reference program's by a relative error of at most 0.005.
Values may be sent and summed in bfloat16 or wider, within the bound.
No kernel may reach another device: no remote copies, remote signals or barrier semaphores. Data moves between devices by JAX's collectives and lax.ppermute only.
A program may use at most 128 MiB of HBM per device.

```python
import jax
import jax.numpy as jnp
from jax import lax

H = 32
HD = 64
Q_DEV = 128
RATIO = 4
G = 32
HK = 2048
E_DEV = 512
Q_TOK = 1024
E_TOK = 4096
NEX = 32
BATCHES = 2
REACH = 128
N_SEQ = 8


def offsets_for(base_key, salt_num, step_rows):
    folded = jax.random.fold_in(base_key, salt_num)
    first_key, second_key = jax.random.split(folded)
    jitter = jax.random.randint(first_key, (BATCHES, NEX + 1), 0, step_rows // 2 + 1)
    forced = jax.random.randint(second_key, (BATCHES, 1), 0, NEX - 1)
    places = jnp.arange(NEX + 1, dtype=jnp.int32)[None, :]
    jitter = jnp.where(places == forced, 0, jitter)
    jitter = jnp.where(places == forced + 1, step_rows // 2, jitter)
    jitter = jnp.where((places == 0) | (places == NEX), 0, jitter)
    return (places * step_rows + jitter).astype(jnp.int32)


def key_values(base_key):
    folded = jax.random.fold_in(base_key, 31)
    values = jax.random.truncated_normal(folded, -4.0, 4.0, (BATCHES, E_TOK, HK), jnp.float32)
    return values


def draw_enc_key(key, part):
    return key_values(key).astype(jnp.bfloat16)


def draw_dec_query(key, part):
    folded = jax.random.fold_in(key, 41)
    values = 0.125 * jax.random.truncated_normal(folded, -4.0, 4.0, (BATCHES, Q_TOK, HK), jnp.float32)
    return values.astype(jnp.bfloat16)


def draw_dec_start(key, part):
    return offsets_for(key, 11, G)


def draw_enc_start(key, part):
    return offsets_for(key, 12, RATIO * G)


def level_of(key, dims, cuts, low, high):
    factor_of = 1.0
    for position, parts in cuts:
        steps = jax.random.uniform(jax.random.fold_in(jax.random.fold_in(key, 6), position), (parts,), jnp.float32, low / len(cuts), high / len(cuts))
        factor_of = factor_of * jnp.repeat(jnp.exp(steps), dims[position] // parts).reshape((-1,) + (1,) * (len(dims) - 1 - position))
    return factor_of


def bell_draw(own_key, dims, deviation, most, pieces=(), kind=jnp.bfloat16):
    drawn = deviation * jax.random.normal(own_key, dims, jnp.float32)
    if pieces:
        drawn = drawn * level_of(own_key, dims, pieces, -0.22, 0.18)
    return jnp.clip(drawn, -most, most).astype(kind)


def setup_inputs(seed: int = 0, part: int = 0) -> dict:
    splits = jax.random.split(jax.random.key(seed), 8)
    own_keys = jax.random.split(jax.random.fold_in(splits[7], part), 8)
    return {
        "dec_query": draw_dec_query(jax.random.fold_in(jax.random.fold_in(splits[7], part), 71), part),
        "enc_key": draw_enc_key(jax.random.fold_in(jax.random.fold_in(splits[7], part), 71), part),
        "enc_value": bell_draw(own_keys[2], (BATCHES, E_TOK, HK), 1.0, 6.0, ((0, 2), (1, 8))),
        "saved_out": bell_draw(own_keys[3], (BATCHES, Q_TOK, HK), 0.5, 3.0, ((0, 2), (1, 8))),
        "d_out": bell_draw(own_keys[4], (BATCHES, Q_TOK, HK), 4.0, 24.0, ((0, 2), (1, 8))),
        "dec_start": draw_dec_start(jax.random.fold_in(jax.random.fold_in(splits[7], part), 71), part),
        "enc_start": draw_enc_start(jax.random.fold_in(jax.random.fold_in(splits[7], part), 71), part),
    }


masked_low = -1e30


def example_ids(positions, starts, total):
    counts = jnp.sum((positions[:, None] >= starts[None, 1:-1]).astype(jnp.int32), axis=1)
    inside = (positions >= 0) & (positions < total)
    return jnp.where(inside, counts, -1).astype(jnp.int32)


def round_low(values):
    low_copy = values.astype(jnp.bfloat16)
    low_copy = lax.optimization_barrier(low_copy)
    return low_copy.astype(jnp.float32)


def window_grads(queries, keys_win, values_win, outputs, grads_out, query_ids, key_ids):
    query_f = queries.astype(jnp.float32)
    key_f = keys_win.astype(jnp.float32)
    value_f = values_win.astype(jnp.float32)
    grad_f = grads_out.astype(jnp.float32)
    output_f = outputs.astype(jnp.float32)
    scores = jnp.einsum("qhd,khd->hqk", query_f, key_f)
    allowed = (query_ids[:, None] == key_ids[None, :])[None]
    masked = jnp.where(allowed, scores, masked_low)
    row_max = jnp.max(masked, axis=2, keepdims=True)
    summed = jnp.sum(jnp.where(allowed, jnp.exp(masked - row_max), 0.0), axis=2, keepdims=True)
    log_total = row_max + jnp.log(summed)
    weights = jnp.where(allowed, jnp.exp(masked - log_total), 0.0)
    weights_low = round_low(weights)
    out_dot = jnp.sum(grad_f * output_f, axis=2).T[:, :, None]
    d_probs = jnp.einsum("qhd,khd->hqk", grad_f, value_f)
    d_scores = round_low(weights * (d_probs - out_dot))
    grad_query = jnp.einsum("hqk,khd->qhd", d_scores, key_f)
    grad_key = jnp.einsum("hqk,qhd->khd", d_scores, query_f)
    grad_value = jnp.einsum("hqk,qhd->khd", weights_low, grad_f)
    return grad_query, grad_key, grad_value


def reference(dec_query, enc_key, enc_value, saved_out, d_out, dec_start, enc_start):
    rim_rows = REACH
    window_rows = E_DEV + 2 * rim_rows
    query_list = []
    key_list = []
    value_list = []
    for batch_idx in range(BATCHES):
        key_pos = jnp.arange(E_TOK + 2 * rim_rows, dtype=jnp.int32) - rim_rows
        key_ids = example_ids(key_pos, enc_start[batch_idx], E_TOK)
        query_ids = example_ids(jnp.arange(Q_TOK, dtype=jnp.int32), dec_start[batch_idx], Q_TOK)
        keys_pad = jnp.pad(enc_key[batch_idx], ((rim_rows, rim_rows), (0, 0)))
        values_pad = jnp.pad(enc_value[batch_idx], ((rim_rows, rim_rows), (0, 0)))
        queries_all = dec_query[batch_idx]
        outputs_all = saved_out[batch_idx]
        grads_all = d_out[batch_idx]

        def shard_step(running, shard_idx):
            key_acc, value_acc = running
            q_start = (shard_idx * Q_DEV).astype(jnp.int32)
            k_start = (shard_idx * E_DEV).astype(jnp.int32)
            queries = lax.dynamic_slice_in_dim(queries_all, q_start, Q_DEV, 0).reshape(Q_DEV, H, HD)
            outputs = lax.dynamic_slice_in_dim(outputs_all, q_start, Q_DEV, 0).reshape(Q_DEV, H, HD)
            grads_out = lax.dynamic_slice_in_dim(grads_all, q_start, Q_DEV, 0).reshape(Q_DEV, H, HD)
            keys_win = lax.dynamic_slice_in_dim(keys_pad, k_start, window_rows, 0).reshape(window_rows, H, HD)
            values_win = lax.dynamic_slice_in_dim(values_pad, k_start, window_rows, 0).reshape(window_rows, H, HD)
            q_ids = lax.dynamic_slice_in_dim(query_ids, q_start, Q_DEV, 0)
            k_ids = lax.dynamic_slice_in_dim(key_ids, k_start, window_rows, 0)
            grad_query, grad_key, grad_value = window_grads(queries, keys_win, values_win, outputs, grads_out, q_ids, k_ids)
            old_key = lax.dynamic_slice_in_dim(key_acc, k_start, window_rows, 0)
            key_acc = lax.dynamic_update_slice_in_dim(key_acc, old_key + grad_key.reshape(window_rows, HK), k_start, 0)
            old_value = lax.dynamic_slice_in_dim(value_acc, k_start, window_rows, 0)
            value_acc = lax.dynamic_update_slice_in_dim(value_acc, old_value + grad_value.reshape(window_rows, HK), k_start, 0)
            return (key_acc, value_acc), grad_query.reshape(Q_DEV, HK).astype(jnp.bfloat16)

        start_acc = jnp.zeros((E_TOK + 2 * rim_rows, HK), jnp.float32)
        (key_acc, value_acc), query_rows = lax.scan(shard_step, (start_acc, start_acc), jnp.arange(N_SEQ, dtype=jnp.int32))
        query_list.append(query_rows.reshape(Q_TOK, HK))
        key_list.append(key_acc[rim_rows:rim_rows + E_TOK].astype(jnp.bfloat16))
        value_list.append(value_acc[rim_rows:rim_rows + E_TOK].astype(jnp.bfloat16))
    return (jnp.stack(query_list), jnp.stack(key_list), jnp.stack(value_list))
```

```python
import functools

import jax
import jax.numpy as jnp
from jax import lax
from jax.experimental import pallas as pl
from jax.experimental.pallas import tpu as pltpu
from jax.sharding import PartitionSpec as P

H = 32
HD = 64
LANES = 256
PER = LANES // HD

low = -1e30
high = 1e30


def dot_nt(a, b):
    return lax.dot_general(a, b, (((1,), (1,)), ((), ())), preferred_element_type=jnp.float32)


def dot_nn(a, b):
    return lax.dot_general(a, b, (((1,), (0,)), ((), ())), preferred_element_type=jnp.float32)


def dot_tn(a, b):
    return lax.dot_general(a, b, (((0,), (0,)), ((), ())), preferred_element_type=jnp.float32)


def spread(rows):
    head = lax.broadcasted_iota(jnp.int32, rows.shape, 1) // HD
    return jnp.concatenate([jnp.where(head == h, rows, jnp.zeros_like(rows)) for h in range(PER)], axis=0)


def gather_heads(full):
    slots = full.shape[0] // PER
    head = lax.broadcasted_iota(jnp.int32, (slots, full.shape[1]), 1) // HD
    out = full[:slots]
    for h in range(1, PER):
        out = jnp.where(head == h, full[h * slots : (h + 1) * slots], out)
    return out


def slot_of(slots):
    return lax.rem(lax.broadcasted_iota(jnp.int32, (1, PER * slots), 1), slots)


def row_dots(outs, spread_grads):
    slots = outs.shape[0]
    full = dot_nt(outs, spread_grads)
    row = lax.broadcasted_iota(jnp.int32, full.shape, 0)
    lane = lax.rem(lax.broadcasted_iota(jnp.int32, full.shape, 1), slots)
    return jnp.sum(jnp.where(row == lane, full, 0.0), axis=0, keepdims=True)


def log_add(a, b):
    top = jnp.maximum(a, b)
    return top + jnp.log(jnp.exp(a - top) + jnp.exp(b - top))


def row_ids(rows, lanes):
    return lax.broadcasted_iota(jnp.int32, (rows, lanes), 0)


def interior_kernel(n_ex, gq, gk, start_ref, q_ref, o_ref, g_ref, k_ref, v_ref, dq_ref, dk_ref, dv_ref, dqe_ref, dke_ref, dve_ref):
    slots = 2 * gq
    win = gk + gk // 2
    slot = slot_of(slots)
    for c in range(q_ref.shape[1] // LANES):
        cols = slice(c * LANES, (c + 1) * LANES)
        parts = []
        for i in range(n_ex - 1):
            q0, k0 = i * gq, i * gk
            d_lo, d_hi = start_ref[0, i] - q0, start_ref[0, i + 1] - q0
            e_lo, e_hi = start_ref[1, i] - k0, start_ref[1, i + 1] - k0
            keys = k_ref[k0 : k0 + win, cols]
            vals = v_ref[k0 : k0 + win, cols]
            qs = spread(q_ref[q0 : q0 + slots, cols])
            gs = spread(g_ref[q0 : q0 + slots, cols])
            s = dot_nt(keys, qs)
            row = row_ids(win, LANES)
            s = jnp.where((row >= e_lo) & (row < e_hi), s, low)
            top = jnp.max(s, axis=0, keepdims=True)
            e = jnp.exp(s - top)
            total = jnp.sum(e, axis=0, keepdims=True)
            inv = jnp.where((slot >= d_lo) & (slot < d_hi), 1.0 / total, 0.0)
            p = e * inv
            dots = row_dots(o_ref[q0 : q0 + slots, cols], gs)
            dp = dot_nt(vals, gs)
            ds = (p * (dp - dots)).astype(jnp.bfloat16)
            dv = dot_nn(p.astype(jnp.bfloat16), gs)
            dk = dot_nn(ds, qs)
            dq = gather_heads(dot_tn(ds, keys))
            parts.append((dq, dk, dv))
        edge = gk // 2
        for which, (ref, ext) in enumerate(((dk_ref, dke_ref), (dv_ref, dve_ref))):
            for i in range(n_ex - 1):
                part = parts[i][1 + which]
                first = part[:edge]
                if i > 0:
                    first = first + parts[i - 1][1 + which][gk:]
                first = first.astype(ref.dtype)
                ref[i * gk : i * gk + edge, cols] = first
                ref[i * gk + edge : (i + 1) * gk, cols] = part[edge:gk].astype(ref.dtype)
                if i == 0:
                    ext[:edge, cols] = first
            tail = parts[n_ex - 2][1 + which][gk:].astype(ref.dtype)
            ext[edge : 2 * edge, cols] = tail
        for i in range(n_ex):
            piece = None
            if i < n_ex - 1:
                piece = parts[i][0][:gq]
            if i > 0:
                other = parts[i - 1][0][gq:]
                piece = other if piece is None else piece + other
            piece = piece.astype(dq_ref.dtype)
            dq_ref[i * gq : (i + 1) * gq, cols] = piece
            if i == 0:
                dqe_ref[:gq, cols] = piece
            if i == n_ex - 1:
                dqe_ref[gq:, cols] = piece


def own_scores(keys_a, keys_b, qs, start_ref, n_ex, gq, gk, swap):
    slots = 2 * gq
    sa = dot_nt(keys_a, qs)
    sb = dot_nt(keys_b, qs)
    slot_a = lax.rem(lax.broadcasted_iota(jnp.int32, sa.shape, 1), slots)
    slot_b = lax.rem(lax.broadcasted_iota(jnp.int32, sb.shape, 1), slots)
    in_a = slot_a >= gq if swap else slot_a < gq
    in_b = slot_b < gq if swap else slot_b >= gq
    a_lo = start_ref[1, n_ex - 1] - (n_ex - 1) * gk
    b_hi = start_ref[1, 0]
    sa = jnp.where(in_a & (row_ids(*sa.shape) >= a_lo), sa, low)
    sb = jnp.where(in_b & (row_ids(*sb.shape) < b_hi), sb, low)
    return sa, sb


def log_sum(sa, sb):
    top = jnp.maximum(jnp.max(sa, axis=0, keepdims=True), jnp.max(sb, axis=0, keepdims=True))
    total = jnp.sum(jnp.exp(sa - top), axis=0, keepdims=True) + jnp.sum(jnp.exp(sb - top), axis=0, keepdims=True)
    return top + jnp.log(total)


def stats_kernel(n_ex, gq, gk, start_ref, qa_ref, qb_ref, oa_ref, ob_ref, ga_ref, gb_ref, ka_ref, kb_ref, stat_ref):
    for c in range(qa_ref.shape[1] // LANES):
        cols = slice(c * LANES, (c + 1) * LANES)
        qs = spread(jnp.concatenate([qa_ref[:, cols], qb_ref[:, cols]], axis=0))
        gs = spread(jnp.concatenate([ga_ref[:, cols], gb_ref[:, cols]], axis=0))
        sa, sb = own_scores(ka_ref[:, cols], kb_ref[:, cols], qs, start_ref, n_ex, gq, gk, False)
        stat_ref[0:1, cols] = log_sum(sa, sb)
        stat_ref[1:2, cols] = row_dots(jnp.concatenate([oa_ref[:, cols], ob_ref[:, cols]], axis=0), gs)


def pick(flag, a, b):
    return jnp.where(flag, a, b)


def remote_kernel(n_ex, gq, gk, start_ref, re_ref, ro_ref, te_ref, to_ref, ka_ref, kb_ref, va_ref, vb_ref, me_ref, mo_ref, stat_ref):
    slots = 2 * gq
    even = start_ref[0, n_ex + 1] == 0
    slot = slot_of(slots)
    for c in range(re_ref.shape[1] // LANES):
        cols = slice(c * LANES, (c + 1) * LANES)
        re, ro = re_ref[:, cols], ro_ref[:, cols]
        before, after = pick(even, ro, re), pick(even, re, ro)
        te, to = te_ref[:, cols], to_ref[:, cols]
        tbefore, tafter = pick(even, to, te), pick(even, te, to)
        stat = jnp.where(slot < gq, tbefore, tafter)
        qs = spread(jnp.concatenate([before[:gq], after[:gq]], axis=0))
        gs = spread(jnp.concatenate([before[gq:], after[gq:]], axis=0))
        keys_a, keys_b = ka_ref[:, cols], kb_ref[:, cols]
        sa, sb = own_scores(keys_a, keys_b, qs, start_ref, n_ex, gq, gk, True)
        mine = log_sum(sa, sb)
        d_lo = start_ref[0, n_ex + 2]
        d_hi = start_ref[0, n_ex] - n_ex * gq + gq
        whole = jnp.where((slot >= d_lo) & (slot < d_hi), log_add(mine, stat[0:1]), high)
        dots = stat[1:2]
        dsa = (jnp.exp(sa - whole) * (dot_nt(va_ref[:, cols], gs) - dots)).astype(jnp.bfloat16)
        dsb = (jnp.exp(sb - whole) * (dot_nt(vb_ref[:, cols], gs) - dots)).astype(jnp.bfloat16)
        dq = gather_heads(dot_tn(dsa, keys_a) + dot_tn(dsb, keys_b)).astype(jnp.bfloat16)
        hi = mine.astype(jnp.bfloat16)
        rest = mine - hi.astype(jnp.float32)
        mid = rest.astype(jnp.bfloat16)
        tail = (rest - mid.astype(jnp.float32)).astype(jnp.bfloat16)
        three = lax.broadcasted_iota(jnp.int32, (16, LANES), 0)
        logs = jnp.where(
            three == 0, hi.astype(jnp.float32), jnp.where(three == 1, mid.astype(jnp.float32), tail.astype(jnp.float32))
        ).astype(jnp.bfloat16)
        to_before, to_after = dq[:gq], dq[gq:]
        me_ref[:gq, cols] = pick(even, to_after, to_before)
        mo_ref[:gq, cols] = pick(even, to_before, to_after)
        me_ref[gq:, cols] = logs
        mo_ref[gq:, cols] = logs
        stat_ref[0:1, cols] = whole
        stat_ref[1:2, cols] = dots


def edge_kernel(
    n_ex, gq, gk, start_ref, re_ref, ro_ref, me_ref, mo_ref, own_ref, far_ref, qa_ref, qb_ref, ga_ref, gb_ref,
    ka_ref, kb_ref, va_ref, vb_ref, dqe_ref, dke_ref, dve_ref, dq_in, dk_in, dv_in, dq_out, dk_out, dv_out,
    dq_buf, dk_buf, dv_buf, sems,
):
    slots = 2 * gq
    edge = gk // 2
    even = start_ref[0, n_ex + 1] == 0
    has_next = start_ref[1, n_ex + 1] == 1
    slot = slot_of(slots)
    width = re_ref.shape[1]
    step = pl.program_id(0)
    for c in range(width // LANES):
        cols = slice(c * LANES, (c + 1) * LANES)
        re, ro = re_ref[:, cols], ro_ref[:, cols]
        before, after = pick(even, ro, re), pick(even, re, ro)
        me, mo = me_ref[:, cols].astype(jnp.float32), mo_ref[:, cols].astype(jnp.float32)
        mbefore, mafter = pick(even, mo, me), pick(even, me, mo)
        log_before = mbefore[gq : gq + 1] + mbefore[gq + 1 : gq + 2] + mbefore[gq + 2 : gq + 3]
        log_after = mafter[gq : gq + 1] + mafter[gq + 1 : gq + 2] + mafter[gq + 2 : gq + 3]
        log_after = jnp.where(has_next, log_after, low)
        own = log_add(own_ref[0:1, cols], jnp.where(slot < gq, log_after, log_before))
        a_lo = start_ref[0, n_ex - 1] - (n_ex - 1) * gq
        b_hi = start_ref[0, 0] + gq
        own = jnp.where((slot >= a_lo) & (slot < b_hi), own, high)
        far = far_ref[0:1, cols]
        own_d, far_d = own_ref[1:2, cols], far_ref[1:2, cols]
        qa, qb, ga, gb = qa_ref[:, cols], qb_ref[:, cols], ga_ref[:, cols], gb_ref[:, cols]
        sides = (
            (qa, after[:gq], ga, after[gq:], ka_ref, va_ref, own, far, own_d, far_d),
            (before[:gq], qb, before[gq:], gb, kb_ref, vb_ref, far, own, far_d, own_d),
        )
        done = []
        for side, (q_1, q_2, g_1, g_2, k_ref, v_ref, log_1, log_2, d_1, d_2) in enumerate(sides):
            qs = spread(jnp.concatenate([q_1, q_2], axis=0))
            gs = spread(jnp.concatenate([g_1, g_2], axis=0))
            whole = jnp.where(slot < gq, log_1, log_2)
            dots = jnp.where(slot < gq, d_1, d_2)
            keys = k_ref[:, cols]
            s = dot_nt(keys, qs)
            row = row_ids(*s.shape)
            if side == 0:
                s = jnp.where(row >= start_ref[1, n_ex - 1] - (n_ex - 1) * gk, s, low)
            else:
                s = jnp.where(row < start_ref[1, 0], s, low)
            p = jnp.exp(s - whole)
            ds = (p * (dot_nt(v_ref[:, cols], gs) - dots)).astype(jnp.bfloat16)
            dv = dot_nn(p.astype(jnp.bfloat16), gs)
            dk = dot_nn(ds, qs)
            dq = gather_heads(dot_tn(ds, keys))
            done.append((dq, dk, dv))
        wide = pl.ds(pl.multiple_of(step * width, width) + c * LANES, LANES)
        f32 = jnp.float32
        for which, (buf, ext) in enumerate(((dk_buf, dke_ref), (dv_buf, dve_ref))):
            part_r, part_l = done[0][1 + which], done[1][1 + which]
            buf[:edge, wide] = (part_l + ext[:edge, cols].astype(f32)).astype(buf.dtype)
            buf[edge : 2 * edge, wide] = (part_r[:edge] + ext[edge:, cols].astype(f32)).astype(buf.dtype)
            buf[2 * edge :, wide] = part_r[edge:].astype(buf.dtype)
        dq_a = done[0][0][:gq] + mafter[:gq] + dqe_ref[gq:, cols].astype(f32)
        half = gq // 2
        dq_b = done[1][0][gq:] + mbefore[:gq] + dqe_ref[:gq, cols].astype(f32)
        dq_buf[:gq, wide] = dq_b.astype(dq_buf.dtype)
        dq_buf[gq:, wide] = dq_a.astype(dq_buf.dtype)

    def copies(at):
        cols = pl.ds(pl.multiple_of(at * width, width), width)
        last = (n_ex - 1) * gk
        out = []
        for j, (buf, ref) in enumerate(((dk_buf, dk_out), (dv_buf, dv_out))):
            out.append(pltpu.make_async_copy(buf.at[pl.ds(0, edge), cols], ref.at[pl.ds(0, edge), cols], sems.at[at, 2 * j]))
            out.append(pltpu.make_async_copy(buf.at[pl.ds(edge, gk), cols], ref.at[pl.ds(last, gk), cols], sems.at[at, 2 * j + 1]))
        out.append(pltpu.make_async_copy(dq_buf.at[pl.ds(0, gq), cols], dq_out.at[pl.ds(0, gq), cols], sems.at[at, 4]))
        out.append(pltpu.make_async_copy(dq_buf.at[pl.ds(gq, gq), cols], dq_out.at[pl.ds((n_ex - 1) * gq, gq), cols], sems.at[at, 5]))
        return out

    for copy in copies(step):
        copy.start()

    @pl.when(step == pl.num_programs(0) - 1)
    def _():
        for at in range(dk_buf.shape[1] // width):
            for copy in copies(at):
                copy.wait()


def call(kernel, steps, width, ins, outs, scratch=(), aliases=None, flops=0, nbytes=0):
    def spec(entry):
        if entry is None:
            return pl.BlockSpec(memory_space=pl.ANY)
        rows, index = entry
        return pl.BlockSpec((rows, width), lambda g, s, index=index: (index, g))

    return pl.pallas_call(
        kernel,
        out_shape=[shape for _, shape in outs],
        grid_spec=pltpu.PrefetchScalarGridSpec(
            num_scalar_prefetch=1,
            grid=(steps,),
            in_specs=[spec(entry) for entry in ins],
            out_specs=[spec(entry) for entry, _ in outs],
            scratch_shapes=list(scratch),
        ),
        input_output_aliases=aliases or {},
        compiler_params=pltpu.CompilerParams(dimension_semantics=("arbitrary",), vmem_limit_bytes=40 * 1024 * 1024),
        cost_estimate=pl.CostEstimate(flops=flops, bytes_accessed=nbytes, transcendentals=0),
    )


def shards(dec_query, enc_key, enc_value, saved_out, d_out, dec_start, enc_start):
    q, k, v, o, g = dec_query[0], enc_key[0], enc_value[0], saved_out[0], d_out[0]
    q_rows, feats = q.shape
    k_rows = k.shape[0]
    pos = lax.axis_index("seq")
    count = lax.axis_size("seq")
    n_ex = (dec_start.shape[1] - 1) // count
    gq, gk = q_rows // n_ex, k_rows // n_ex
    edge = gk // 2
    even = lax.rem(pos, 2) == 0
    bf16, f32 = jnp.bfloat16, jnp.float32

    def swap_even(x):
        return lax.ppermute(x, "seq", [(i, i ^ 1) for i in range(count) if i ^ 1 < count])

    def swap_odd(x):
        pairs = []
        for i in range(1, count - 1, 2):
            pairs += [(i, i + 1), (i + 1, i)]
        return lax.ppermute(x, "seq", pairs)

    starts = jnp.concatenate([dec_start, enc_start], axis=0)
    rows = jnp.array([q_rows, k_rows], jnp.int32)
    near = lax.dynamic_slice(starts, (0, pos * n_ex), (2, n_ex + 1)) - pos * rows[:, None]
    prior = lax.dynamic_slice(starts, (0, jnp.maximum(pos * n_ex - 1, 0)), (1, 1))[0, 0] - pos * q_rows + gq
    prior = jnp.where(pos > 0, prior, gq)
    extra = jnp.stack([lax.rem(pos, 2), prior, (pos < count - 1).astype(jnp.int32), jnp.int32(0)]).reshape(2, 2)
    table = jnp.concatenate([near, extra.astype(jnp.int32)], axis=1)

    last = (n_ex - 1) * gq
    at_e, at_o = jnp.where(even, last, 0), jnp.where(even, 0, last)

    def message(at):
        return jnp.concatenate([lax.dynamic_slice(q, (at, 0), (gq, feats)), lax.dynamic_slice(g, (at, 0), (gq, feats))], axis=0)

    raw_e = swap_even(message(at_e))
    raw_o = swap_odd(message(at_o))

    width = 512
    steps = feats // width
    stat_shape = jax.ShapeDtypeStruct((2, feats), f32)
    a_q, b_q = (gq, n_ex - 1), (gq, 0)
    a_k, b_k = (gk, n_ex - 1), (edge, 0)
    (own,) = call(
        functools.partial(stats_kernel, n_ex, gq, gk), steps, width,
        [a_q, b_q, a_q, b_q, a_q, b_q, a_k, b_k],
        [((2, 0), stat_shape)], flops=int(4e8), nbytes=int(2e6),
    )(table, q, q, o, o, g, g, k, k)
    stat_e = swap_even(own)
    stat_o = swap_odd(own)

    msg_shape = jax.ShapeDtypeStruct((gq + 16, feats), bf16)
    raw = (2 * gq, 0)
    stat = (2, 0)
    msg = (gq + 16, 0)
    to_e, to_o, far = call(
        functools.partial(remote_kernel, n_ex, gq, gk), steps, width,
        [raw, raw, stat, stat, a_k, b_k, a_k, b_k],
        [(msg, msg_shape), (msg, msg_shape), (stat, stat_shape)], flops=int(8e8), nbytes=int(3e6),
    )(table, raw_e, raw_o, stat_e, stat_o, k, k, v, v)
    back_e = swap_even(to_e)
    back_o = swap_odd(to_o)

    full_q, full_k = (q_rows, 0), (k_rows, 0)
    q_shape, k_shape = jax.ShapeDtypeStruct(q.shape, bf16), jax.ShapeDtypeStruct(k.shape, bf16)
    dq, dk, dv, dqe, dke, dve = call(
        functools.partial(interior_kernel, n_ex, gq, gk), steps, width,
        [full_q, full_q, full_q, full_k, full_k],
        [
            (full_q, q_shape), (full_k, k_shape), (full_k, k_shape),
            ((2 * gq, 0), jax.ShapeDtypeStruct((2 * gq, feats), bf16)),
            ((gk, 0), jax.ShapeDtypeStruct((gk, feats), bf16)),
            ((gk, 0), jax.ShapeDtypeStruct((gk, feats), bf16)),
        ],
        flops=int(4e9), nbytes=int(11e6),
    )(table, q, o, g, k, v)

    dq, dk, dv = call(
        functools.partial(edge_kernel, n_ex, gq, gk), steps, width,
        [raw, raw, msg, msg, stat, stat, a_q, b_q, a_q, b_q, a_k, b_k, a_k, b_k, (2 * gq, 0), (gk, 0), (gk, 0), None, None, None],
        [(None, q_shape), (None, k_shape), (None, k_shape)],
        scratch=[
            pltpu.VMEM((2 * gq, feats), bf16), pltpu.VMEM((gk + edge, feats), bf16), pltpu.VMEM((gk + edge, feats), bf16),
            pltpu.SemaphoreType.DMA((steps, 6)),
        ],
        aliases={18: 0, 19: 1, 20: 2},
        flops=int(1e9), nbytes=int(6e6),
    )(table, raw_e, raw_o, back_e, back_o, own, far, q, q, g, g, k, k, v, v, dqe, dke, dve, dq, dk, dv)
    return dq[None], dk[None], dv[None]


def solution(mesh):
    spec = P(("grp", "dp"), "seq", None)
    return jax.shard_map(
        shards,
        mesh=mesh,
        in_specs=(spec,) * 5 + (P(("grp", "dp"), None),) * 2,
        out_specs=(spec,) * 3,
        check_vma=False,
    )
```

```python
import functools

import jax
import jax.numpy as jnp
from jax import lax
from jax.experimental import pallas as pl
from jax.experimental.pallas import tpu as pltpu
from jax.sharding import PartitionSpec as P

H = 32
HD = 64
LANES = 256
PER = LANES // HD

low = -1e30
high = 1e30
BATCH = 2
SPLIT = 4


def dot_nt(a, b):
    return lax.dot_general(a, b, (((1,), (1,)), ((), ())), preferred_element_type=jnp.float32)


def dot_nn(a, b):
    return lax.dot_general(a, b, (((1,), (0,)), ((), ())), preferred_element_type=jnp.float32)


def dot_tn(a, b):
    return lax.dot_general(a, b, (((0,), (0,)), ((), ())), preferred_element_type=jnp.float32)


def spread(rows):
    head = lax.broadcasted_iota(jnp.int32, rows.shape, 1) // HD
    return jnp.concatenate([jnp.where(head == h, rows, jnp.zeros_like(rows)) for h in range(PER)], axis=0)


def gather_heads(full):
    slots = full.shape[0] // PER
    head = lax.broadcasted_iota(jnp.int32, (slots, full.shape[1]), 1) // HD
    out = full[:slots]
    for h in range(1, PER):
        out = jnp.where(head == h, full[h * slots : (h + 1) * slots], out)
    return out


def slot_of(slots):
    return lax.rem(lax.broadcasted_iota(jnp.int32, (1, PER * slots), 1), slots)


def row_dots(outs, spread_grads):
    slots = outs.shape[0]
    full = dot_nt(outs, spread_grads)
    row = lax.broadcasted_iota(jnp.int32, full.shape, 0)
    lane = lax.rem(lax.broadcasted_iota(jnp.int32, full.shape, 1), slots)
    return jnp.sum(jnp.where(row == lane, full, 0.0), axis=0, keepdims=True)


def log_add(a, b):
    top = jnp.maximum(a, b)
    return top + jnp.log(jnp.exp(a - top) + jnp.exp(b - top))


def row_ids(rows, lanes):
    return lax.broadcasted_iota(jnp.int32, (rows, lanes), 0)


def run_skewed(units):
    live, queue = [], list(units)
    while queue or live:
        if queue:
            live.append(queue.pop(0))
        for unit in list(live):
            try:
                next(unit)
            except StopIteration:
                live.remove(unit)


def each_group(groups, batch, units_of):
    @pl.loop(0, groups // batch)
    def _(at):
        units = []
        for c in range(batch):
            start = at * (batch * LANES) + c * LANES
            units += units_of(pl.ds(pl.multiple_of(start, LANES), LANES))
        run_skewed(units)


class Bounds:
    def __init__(self, shape, table):
        self.n_ex, self.gq, self.gk, self.count = shape
        self.dec_ref, self.enc_ref, pos_ref = table
        self.pos = pos_ref[0]
        self.even = lax.rem(self.pos, 2) == 0
        self.has_next = self.pos < self.count - 1

    def dec(self, i):
        return self.dec_ref[0, self.pos * self.n_ex + i] - self.pos * (self.n_ex * self.gq)

    def enc(self, i):
        return self.enc_ref[0, self.pos * self.n_ex + i] - self.pos * (self.n_ex * self.gk)

    def prior(self):
        at = jnp.maximum(self.pos * self.n_ex - 1, 0)
        rows = self.dec_ref[0, at] - self.pos * (self.n_ex * self.gq) + self.gq
        return jnp.where(self.pos > 0, rows, self.gq)

    def far_lanes(self, slot):
        hi = self.dec(self.n_ex) - self.n_ex * self.gq + self.gq
        return (slot >= self.prior()) & (slot < hi)

    def own_lanes(self, slot):
        lo = self.dec(self.n_ex - 1) - (self.n_ex - 1) * self.gq
        return (slot >= lo) & (slot < self.dec(0) + self.gq)


def edge_mask(bounds, s, far):
    gq, gk = bounds.gq, bounds.gk
    edge = gk // 2
    slot = slot_of(2 * gq)
    first = slot < gq
    in_a, in_b = (~first, first) if far else (first, ~first)
    row = row_ids(edge, LANES)
    a_lo = bounds.enc(bounds.n_ex - 1) - (bounds.n_ex - 1) * gk
    s0 = jnp.where(in_a & (row >= a_lo), s[:edge], low)
    s1 = jnp.where(in_a, s[edge:gk], low)
    s2 = jnp.where(in_b & (row < bounds.enc(0)), s[gk:], low)
    return s0, s1, s2


def exp_sum(s0, s1, s2):
    top = jnp.max(jnp.maximum(jnp.maximum(s0, s1), s2), axis=0, keepdims=True)
    e0, e1, e2 = jnp.exp(s0 - top), jnp.exp(s1 - top), jnp.exp(s2 - top)
    return top, e0, e1, e2, jnp.sum(e0 + e1 + e2, axis=0, keepdims=True)


def interior_kernel(shape, lo, hi, *refs):
    table, (_, q_ref, o_ref, g_ref, k_ref, v_ref), refs = refs[:3], refs[3:9], refs[9:]
    if lo > 0:
        refs = refs[6:]
    dq_out, dk_out, dv_out, dqe_ref, dke_ref, dve_ref, dq_buf, dk_buf, dv_buf, sems = refs
    bounds = Bounds(shape, table)
    n_ex, gq, gk = bounds.n_ex, bounds.gq, bounds.gk
    slots = 2 * gq
    edge = gk // 2
    win = gk + edge
    slot = slot_of(slots)
    bf16 = jnp.bfloat16

    def unit(i, cols, held):
        q0, k0 = i * gq, i * gk
        d_lo, d_hi = bounds.dec(i) - q0, bounds.dec(i + 1) - q0
        e_lo, e_hi = bounds.enc(i) - k0, bounds.enc(i + 1) - k0 - gk
        keys = k_ref[k0 : k0 + win, cols]
        qs = spread(q_ref[q0 : q0 + slots, cols])
        s = dot_nt(keys, qs)
        gs = spread(g_ref[q0 : q0 + slots, cols])
        dots = row_dots(o_ref[q0 : q0 + slots, cols], gs)
        dp = dot_nt(v_ref[k0 : k0 + win, cols], gs)
        yield
        row = row_ids(edge, LANES)
        s0 = jnp.where(row >= e_lo, s[:edge], low)
        s2 = jnp.where(row < e_hi, s[gk:], low)
        _, e0, e1, e2, total = exp_sum(s0, s[edge:gk], s2)
        yield
        inv = jnp.where((slot >= d_lo) & (slot < d_hi), 1.0 / total, 0.0)
        p = jnp.concatenate([e0, e1, e2], axis=0) * inv
        p_low = p.astype(bf16)
        yield
        dv = dot_nn(p_low, gs)
        ds = (p * (dp - dots)).astype(bf16)
        yield
        dk = dot_nn(ds, qs)
        dq = gather_heads(dot_tn(ds, keys))
        yield
        for which, (ref, ext, part) in enumerate(((dk_buf, dke_ref, dk), (dv_buf, dve_ref, dv))):
            first = part[:edge]
            if i > 0:
                first = first + held[(i - 1, which)]
                ref[k0 : k0 + edge, cols] = first.astype(bf16)
            else:
                ext[:edge, cols] = first.astype(bf16)
            ref[k0 + edge : k0 + gk, cols] = part[edge:gk].astype(bf16)
            if i < n_ex - 2:
                held[(i, which)] = part[gk:]
            else:
                ext[edge:, cols] = part[gk:].astype(bf16)
        first = dq[:gq]
        if i > 0:
            dq_buf[q0 : q0 + gq, cols] = (first + held[(i - 1, 2)]).astype(bf16)
        else:
            dqe_ref[:gq, cols] = first.astype(bf16)
        if i < n_ex - 2:
            held[(i, 2)] = dq[gq:]
        else:
            dqe_ref[gq:, cols] = dq[gq:].astype(bf16)
        yield

    def copies(at):
        cols = pl.ds(pl.multiple_of(at * (BATCH * LANES), LANES), BATCH * LANES)
        out = []
        k_rows, q_rows = pl.ds(edge, (n_ex - 1) * gk - edge), pl.ds(gq, (n_ex - 2) * gq)
        for j, (buf, ref, rows) in enumerate(((dk_buf, dk_out, k_rows), (dv_buf, dv_out, k_rows), (dq_buf, dq_out, q_rows))):
            out.append(pltpu.make_async_copy(buf.at[rows, cols], ref.at[rows, cols], sems.at[at, j]))
        return out

    @pl.loop(lo // BATCH, hi // BATCH)
    def _(at):
        units = []
        for c in range(BATCH):
            cols = pl.ds(pl.multiple_of(at * (BATCH * LANES) + c * LANES, LANES), LANES)
            held = {}
            units += [unit(i, cols, held) for i in range(n_ex - 1)]
        run_skewed(units)
        for copy in copies(at):
            copy.start()

    @pl.loop(lo // BATCH, hi // BATCH)
    def _(at):
        for copy in copies(at):
            copy.wait()


def stats_kernel(shape, *refs):
    *table, q_hbm, o_hbm, g_hbm, k_hbm, stat_ref, q_ref, o_ref, g_ref, k_ref, sems = refs
    bounds = Bounds(shape, table)
    n_ex, gq, gk = bounds.n_ex, bounds.gq, bounds.gk
    edge = gk // 2
    last = (n_ex - 1) * gq

    def moved(src, dst, rows, sem):
        return pltpu.make_async_copy(src.at[pl.ds(*rows)], dst.at[pl.ds(*rows)], sems.at[sem])

    ends = [
        pltpu.make_async_copy(k_hbm.at[pl.ds((n_ex - 1) * gk, gk)], k_ref.at[pl.ds(0, gk)], sems.at[0]),
        pltpu.make_async_copy(k_hbm.at[pl.ds(0, edge)], k_ref.at[pl.ds(gk, edge)], sems.at[1]),
    ]
    rest = []
    for j, (src, dst) in enumerate(((q_hbm, q_ref), (g_hbm, g_ref), (o_hbm, o_ref))):
        ends.append(moved(src, dst, (last, gq), 3 * j + 2))
        ends.append(moved(src, dst, (0, gq), 3 * j + 3))
        rest.append(moved(src, dst, (gq, last - gq), 3 * j + 4))
    for copy in ends + rest:
        copy.start()
    for copy in ends:
        copy.wait()

    def both(ref, cols):
        return jnp.concatenate([ref[last:, cols], ref[:gq, cols]], axis=0)

    def unit(cols):
        qs = spread(both(q_ref, cols))
        s = dot_nt(k_ref[:, cols], qs)
        yield
        dots = row_dots(both(o_ref, cols), spread(both(g_ref, cols)))
        yield
        top, _, _, _, total = exp_sum(*edge_mask(bounds, s, False))
        stat_ref[0:1, cols] = top + jnp.log(total)
        stat_ref[1:2, cols] = dots
        yield

    each_group(q_ref.shape[1] // LANES, 4, lambda cols: [unit(cols)])
    for copy in rest:
        copy.wait()


def pick(flag, a, b):
    return jnp.where(flag, a, b)


def remote_kernel(shape, *refs):
    *table, _, re_ref, ro_ref, te_ref, to_ref, k_ref, v_ref, me_ref, mo_ref, stat_ref = refs
    bounds = Bounds(shape, table)
    n_ex, gq, gk = bounds.n_ex, bounds.gq, bounds.gk
    edge = gk // 2
    even = bounds.even
    slot = slot_of(2 * gq)
    bf16, f32 = jnp.bfloat16, jnp.float32
    last = (n_ex - 1) * gk

    def ends(ref, cols):
        return jnp.concatenate([ref[last:, cols], ref[:edge, cols]], axis=0)

    def unit(cols):
        re, ro = re_ref[:, cols], ro_ref[:, cols]
        before, after = pick(even, ro, re), pick(even, re, ro)
        qs = spread(jnp.concatenate([before[:gq], after[:gq]], axis=0))
        keys = ends(k_ref, cols)
        s = dot_nt(keys, qs)
        gs = spread(jnp.concatenate([before[gq:], after[gq:]], axis=0))
        dp = dot_nt(ends(v_ref, cols), gs)
        yield
        te, to = te_ref[:, cols], to_ref[:, cols]
        tbefore, tafter = pick(even, to, te), pick(even, te, to)
        stat = jnp.where(slot < gq, tbefore, tafter)
        top, e0, e1, e2, total = exp_sum(*edge_mask(bounds, s, True))
        mine = top + jnp.log(total)
        yield
        whole = log_add(mine, stat[0:1])
        dots = stat[1:2]
        scale = jnp.where(bounds.far_lanes(slot), jnp.exp(top - whole), 0.0)
        p = jnp.concatenate([e0, e1, e2], axis=0) * scale
        ds = (p * (dp - dots)).astype(bf16)
        stat_ref[0:1, cols] = jnp.where(bounds.far_lanes(slot), whole, high)
        stat_ref[1:2, cols] = dots
        yield
        dq = gather_heads(dot_tn(ds, keys)).astype(bf16)
        hi = mine.astype(bf16).astype(f32)
        mid = (mine - hi).astype(bf16).astype(f32)
        tail = mine - hi - mid
        three = lax.broadcasted_iota(jnp.int32, (8, LANES), 0)
        logs = jnp.where(three == 0, hi, jnp.where(three == 1, mid, tail)).astype(bf16)
        yield
        me_ref[:gq, cols] = pick(even, dq[gq:], dq[:gq])
        mo_ref[:gq, cols] = pick(even, dq[:gq], dq[gq:])
        me_ref[gq:, cols] = logs
        mo_ref[gq:, cols] = logs
        yield

    each_group(re_ref.shape[1] // LANES, 4, lambda cols: [unit(cols)])


def edge_kernel(shape, *refs):
    *table, re_ref, ro_ref, me_ref, mo_ref, own_ref, far_ref, q_ref, g_ref, k_ref, v_ref = refs[:13]
    dqe_ref, dke_ref, dve_ref, _, _, _, dq_out, dk_out, dv_out, dq_buf, dk_buf, dv_buf, sems = refs[13:]
    bounds = Bounds(shape, table)
    n_ex, gq, gk = bounds.n_ex, bounds.gq, bounds.gk
    edge = gk // 2
    even = bounds.even
    slot = slot_of(2 * gq)
    bf16, f32 = jnp.bfloat16, jnp.float32
    last_q, last_k = (n_ex - 1) * gq, (n_ex - 1) * gk

    def unit(side, cols):
        far = pick(even, re_ref[:, cols], ro_ref[:, cols]) if side == 0 else pick(even, ro_ref[:, cols], re_ref[:, cols])
        back = (me_ref, mo_ref) if side == 0 else (mo_ref, me_ref)
        if side == 0:
            pieces = [(q_ref[last_q:, cols], far[:gq]), (g_ref[last_q:, cols], far[gq:])]
            keys, vals = k_ref[last_k:, cols], v_ref[last_k:, cols]
        else:
            pieces = [(far[:gq], q_ref[:gq, cols]), (far[gq:], g_ref[:gq, cols])]
            keys, vals = k_ref[:edge, cols], v_ref[:edge, cols]
        qs, gs = (spread(jnp.concatenate(pair, axis=0)) for pair in pieces)
        s = dot_nt(keys, qs)
        dp = dot_nt(vals, gs)
        yield
        logs = pick(even, back[0][gq:, cols].astype(f32), back[1][gq:, cols].astype(f32))
        log_far = logs[0:1] + logs[1:2] + logs[2:3]
        if side == 0:
            log_far = jnp.where(bounds.has_next, log_far, low)
        log_own = log_add(own_ref[0:1, cols], log_far)
        log_own = jnp.where(bounds.own_lanes(slot), log_own, high)
        mine = slot < gq if side == 0 else slot >= gq
        whole = jnp.where(mine, log_own, far_ref[0:1, cols])
        dots = jnp.where(mine, own_ref[1:2, cols], far_ref[1:2, cols])
        row = row_ids(edge, LANES)
        if side == 0:
            s = jnp.concatenate([jnp.where(row >= bounds.enc(n_ex - 1) - last_k, s[:edge], low), s[edge:]], axis=0)
        else:
            s = jnp.where(row < bounds.enc(0), s, low)
        p = jnp.exp(s - whole)
        p_low = p.astype(bf16)
        yield
        dv = dot_nn(p_low, gs)
        ds = (p * (dp - dots)).astype(bf16)
        yield
        dk = dot_nn(ds, qs)
        dq = gather_heads(dot_tn(ds, keys))
        yield
        for buf, ext, part in ((dk_buf, dke_ref, dk), (dv_buf, dve_ref, dv)):
            if side == 0:
                buf[edge:gk, cols] = (part[:edge] + ext[edge:, cols].astype(f32)).astype(bf16)
                buf[gk:, cols] = part[edge:].astype(bf16)
            else:
                buf[:edge, cols] = (part + ext[:edge, cols].astype(f32)).astype(bf16)
        rows = slice(gq, 2 * gq) if side == 0 else slice(0, gq)
        add = pick(even, back[0][:gq, cols].astype(f32), back[1][:gq, cols].astype(f32))
        part = dq[:gq] if side == 0 else dq[gq:]
        dq_buf[rows, cols] = (part + add + dqe_ref[rows, cols].astype(f32)).astype(bf16)
        yield

    def copies(at):
        cols = pl.ds(pl.multiple_of(at * (BATCH * LANES), LANES), BATCH * LANES)
        out = []
        for j, (buf, ref) in enumerate(((dk_buf, dk_out), (dv_buf, dv_out))):
            out.append(pltpu.make_async_copy(buf.at[pl.ds(0, edge), cols], ref.at[pl.ds(0, edge), cols], sems.at[at, 2 * j]))
            out.append(pltpu.make_async_copy(buf.at[pl.ds(edge, gk), cols], ref.at[pl.ds(last_k, gk), cols], sems.at[at, 2 * j + 1]))
        out.append(pltpu.make_async_copy(dq_buf.at[pl.ds(0, gq), cols], dq_out.at[pl.ds(0, gq), cols], sems.at[at, 4]))
        out.append(pltpu.make_async_copy(dq_buf.at[pl.ds(gq, gq), cols], dq_out.at[pl.ds(last_q, gq), cols], sems.at[at, 5]))
        return out

    turns = q_ref.shape[1] // LANES // BATCH

    @pl.loop(0, turns)
    def _(at):
        units = []
        for c in range(BATCH):
            cols = pl.ds(pl.multiple_of(at * (BATCH * LANES) + c * LANES, LANES), LANES)
            units += [unit(0, cols), unit(1, cols)]
        run_skewed(units)
        for copy in copies(at):
            copy.start()

    @pl.loop(0, turns)
    def _(at):
        for copy in copies(at):
            copy.wait()


inside = pl.BlockSpec(memory_space=pltpu.VMEM)
anywhere = pl.BlockSpec(memory_space=pl.ANY)
off_chip = pl.BlockSpec(memory_space=pltpu.HBM)


def call(kernel, ins, outs, scratch=(), aliases=None, flops=0, nbytes=0):
    return pl.pallas_call(
        kernel,
        out_shape=[shape for _, shape in outs],
        in_specs=[pl.BlockSpec(memory_space=pltpu.SMEM)] * 3 + list(ins),
        out_specs=[spec for spec, _ in outs],
        scratch_shapes=list(scratch),
        input_output_aliases=aliases or {},
        compiler_params=pltpu.CompilerParams(vmem_limit_bytes=40 * 1024 * 1024),
        cost_estimate=pl.CostEstimate(flops=flops, bytes_accessed=nbytes, transcendentals=0),
    )


def shards(dec_query, enc_key, enc_value, saved_out, d_out, dec_start, enc_start):
    q, k, v, o, g = dec_query[0], enc_key[0], enc_value[0], saved_out[0], d_out[0]
    q_rows, feats = q.shape
    k_rows = k.shape[0]
    pos = lax.axis_index("seq")
    count = lax.axis_size("seq")
    n_ex = (dec_start.shape[1] - 1) // count
    gq, gk = q_rows // n_ex, k_rows // n_ex
    edge = gk // 2
    groups = feats // LANES
    even = lax.rem(pos, 2) == 0
    bf16, f32 = jnp.bfloat16, jnp.float32
    shape = (n_ex, gq, gk, count)

    def swap_even(x):
        return lax.ppermute(x, "seq", [(i, i ^ 1) for i in range(count) if i ^ 1 < count])

    def swap_odd(x):
        pairs = []
        for i in range(1, count - 1, 2):
            pairs += [(i, i + 1), (i + 1, i)]
        return lax.ppermute(x, "seq", pairs)

    table = (dec_start, enc_start, pos.astype(jnp.int32)[None])
    last = (n_ex - 1) * gq
    at_e, at_o = jnp.where(even, last, 0), jnp.where(even, 0, last)

    def message(at):
        return jnp.concatenate([lax.dynamic_slice(q, (at, 0), (gq, feats)), lax.dynamic_slice(g, (at, 0), (gq, feats))], axis=0)

    raw_e = swap_even(message(at_e))
    raw_o = swap_odd(message(at_o))

    def like(rows, kind=bf16):
        return jax.ShapeDtypeStruct((rows, feats), kind)

    def vmem(rows):
        return pltpu.VMEM((rows, feats), bf16)

    own, q, o, g = call(
        functools.partial(stats_kernel, shape), [off_chip] * 4, [(inside, like(2, f32))] + [(inside, like(q_rows))] * 3,
        scratch=[vmem(gk + edge), pltpu.SemaphoreType.DMA((11,))],
        flops=int(4e8), nbytes=int(2e6),
    )(*table, *(pltpu.with_memory_space_constraint(x, pltpu.HBM) for x in (q, o, g, k)))
    stat_e = swap_even(own)
    stat_o = swap_odd(own)

    def interior(lo, hi, after, before=()):
        return call(
            functools.partial(interior_kernel, shape, lo, hi),
            [anywhere] + [inside] * 5 + ([anywhere] * 3 + [inside] * 3 if before else []),
            [(anywhere, like(q_rows)), (anywhere, like(k_rows)), (anywhere, like(k_rows)),
             (inside, like(2 * gq)), (inside, like(gk)), (inside, like(gk))],
            scratch=[vmem(q_rows), vmem(k_rows), vmem(k_rows), pltpu.SemaphoreType.DMA((groups // BATCH, 3))],
            aliases={9 + j: j for j in range(6)} if before else {},
            flops=int(5e8) * (hi - lo), nbytes=int(1e6) * (hi - lo),
        )(*table, after, q, o, g, k, v, *before)

    part = interior(0, SPLIT, own)
    to_e, to_o, far = call(
        functools.partial(remote_kernel, shape), [anywhere] + [inside] * 6,
        [(inside, like(gq + 8)), (inside, like(gq + 8)), (inside, like(2, f32))],
        flops=int(8e8), nbytes=int(3e6),
    )(*table, part[3], raw_e, raw_o, stat_e, stat_o, k, v)
    back_e = swap_even(to_e)
    back_o = swap_odd(to_o)
    if SPLIT < groups:
        part = interior(SPLIT, groups, far, part)
    dq, dk, dv, dqe, dke, dve = part
    dq, dk, dv = call(
        functools.partial(edge_kernel, shape), [inside] * 13 + [anywhere] * 3,
        [(anywhere, like(q_rows)), (anywhere, like(k_rows)), (anywhere, like(k_rows))],
        scratch=[vmem(2 * gq), vmem(gk + edge), vmem(gk + edge), pltpu.SemaphoreType.DMA((groups // BATCH, 6))],
        aliases={16: 0, 17: 1, 18: 2},
        flops=int(1e9), nbytes=int(6e6),
    )(*table, raw_e, raw_o, back_e, back_o, own, far, q, g, k, v, dqe, dke, dve, dq, dk, dv)
    return dq[None], dk[None], dv[None]


def solution(mesh):
    spec = P(("grp", "dp"), "seq", None)
    return jax.shard_map(
        shards,
        mesh=mesh,
        in_specs=(spec,) * 5 + (P(("grp", "dp"), None),) * 2,
        out_specs=(spec,) * 3,
        check_vma=False,
    )
```

```python
import functools

import jax
import jax.numpy as jnp
from jax import lax
from jax.experimental import pallas as pl
from jax.experimental.pallas import tpu as pltpu
from jax.sharding import PartitionSpec as P

H = 32
HD = 64
LANES = 256
PER = LANES // HD

low = -1e30
high = 1e30
BATCH = 4


def dot_nt(a, b):
    return lax.dot_general(a, b, (((1,), (1,)), ((), ())), preferred_element_type=jnp.float32)


def dot_nn(a, b):
    return lax.dot_general(a, b, (((1,), (0,)), ((), ())), preferred_element_type=jnp.float32)


def dot_tn(a, b):
    return lax.dot_general(a, b, (((0,), (0,)), ((), ())), preferred_element_type=jnp.float32)


def spread(rows):
    head = lax.broadcasted_iota(jnp.int32, rows.shape, 1) // HD
    return jnp.concatenate([jnp.where(head == h, rows, jnp.zeros_like(rows)) for h in range(PER)], axis=0)


def gather_heads(full):
    slots = full.shape[0] // PER
    head = lax.broadcasted_iota(jnp.int32, (slots, full.shape[1]), 1) // HD
    out = full[:slots]
    for h in range(1, PER):
        out = jnp.where(head == h, full[h * slots : (h + 1) * slots], out)
    return out


def slot_of(slots):
    return lax.rem(lax.broadcasted_iota(jnp.int32, (1, PER * slots), 1), slots)


def row_dots(outs, spread_grads):
    slots = outs.shape[0]
    full = dot_nt(outs, spread_grads)
    row = lax.broadcasted_iota(jnp.int32, full.shape, 0)
    lane = lax.rem(lax.broadcasted_iota(jnp.int32, full.shape, 1), slots)
    return jnp.sum(jnp.where(row == lane, full, 0.0), axis=0, keepdims=True)


def log_add(a, b):
    top = jnp.maximum(a, b)
    return top + jnp.log(jnp.exp(a - top) + jnp.exp(b - top))


def row_ids(rows, lanes):
    return lax.broadcasted_iota(jnp.int32, (rows, lanes), 0)


def run_skewed(units):
    live, queue = [], list(units)
    while queue or live:
        if queue:
            live.append(queue.pop(0))
        for unit in list(live):
            try:
                next(unit)
            except StopIteration:
                live.remove(unit)


def each_group(groups, batch, units_of):
    @pl.loop(0, groups // batch)
    def _(at):
        units = []
        for c in range(batch):
            start = at * (batch * LANES) + c * LANES
            units += units_of(pl.ds(pl.multiple_of(start, LANES), LANES))
        run_skewed(units)


class Bounds:
    def __init__(self, shape, table):
        self.n_ex, self.gq, self.gk, self.count = shape
        self.dec_ref, self.enc_ref, pos_ref = table
        self.pos = pos_ref[0]
        self.even = lax.rem(self.pos, 2) == 0
        self.has_next = self.pos < self.count - 1

    def dec(self, i):
        return self.dec_ref[0, self.pos * self.n_ex + i] - self.pos * (self.n_ex * self.gq)

    def enc(self, i):
        return self.enc_ref[0, self.pos * self.n_ex + i] - self.pos * (self.n_ex * self.gk)

    def prior(self):
        at = jnp.maximum(self.pos * self.n_ex - 1, 0)
        rows = self.dec_ref[0, at] - self.pos * (self.n_ex * self.gq) + self.gq
        return jnp.where(self.pos > 0, rows, self.gq)

    def far_lanes(self, slot):
        hi = self.dec(self.n_ex) - self.n_ex * self.gq + self.gq
        return (slot >= self.prior()) & (slot < hi)

    def own_lanes(self, slot):
        lo = self.dec(self.n_ex - 1) - (self.n_ex - 1) * self.gq
        return (slot >= lo) & (slot < self.dec(0) + self.gq)


def edge_mask(bounds, s, far):
    gq, gk = bounds.gq, bounds.gk
    edge = gk // 2
    slot = slot_of(2 * gq)
    first = slot < gq
    in_a, in_b = (~first, first) if far else (first, ~first)
    row = row_ids(edge, LANES)
    a_lo = bounds.enc(bounds.n_ex - 1) - (bounds.n_ex - 1) * gk
    s0 = jnp.where(in_a & (row >= a_lo), s[:edge], low)
    s1 = jnp.where(in_a, s[edge:gk], low)
    s2 = jnp.where(in_b & (row < bounds.enc(0)), s[gk:], low)
    return s0, s1, s2


def exp_sum(s0, s1, s2):
    top = jnp.max(jnp.maximum(jnp.maximum(s0, s1), s2), axis=0, keepdims=True)
    e0, e1, e2 = jnp.exp(s0 - top), jnp.exp(s1 - top), jnp.exp(s2 - top)
    return top, e0, e1, e2, jnp.sum(e0 + e1 + e2, axis=0, keepdims=True)


def interior_kernel(shape, *refs):
    table, (_, q_ref, o_ref, g_ref, k_ref, v_ref), refs = refs[:3], refs[3:9], refs[9:]
    dq_out, dk_out, dv_out, dqe_ref, dke_ref, dve_ref, dq_buf, dk_buf, dv_buf, sems = refs
    bounds = Bounds(shape, table)
    n_ex, gq, gk = bounds.n_ex, bounds.gq, bounds.gk
    slots = 2 * gq
    edge = gk // 2
    win = gk + edge
    slot = slot_of(slots)
    bf16 = jnp.bfloat16

    def unit(i, cols, held):
        q0, k0 = i * gq, i * gk
        d_lo, d_hi = bounds.dec(i) - q0, bounds.dec(i + 1) - q0
        e_lo, e_hi = bounds.enc(i) - k0, bounds.enc(i + 1) - k0 - gk
        keys = k_ref[k0 : k0 + win, cols]
        qs = spread(q_ref[q0 : q0 + slots, cols])
        s = dot_nt(keys, qs)
        gs = spread(g_ref[q0 : q0 + slots, cols])
        dots = row_dots(o_ref[q0 : q0 + slots, cols], gs)
        dp = dot_nt(v_ref[k0 : k0 + win, cols], gs)
        yield
        row = row_ids(edge, LANES)
        s0 = jnp.where(row >= e_lo, s[:edge], low)
        s2 = jnp.where(row < e_hi, s[gk:], low)
        _, e0, e1, e2, total = exp_sum(s0, s[edge:gk], s2)
        yield
        inv = jnp.where((slot >= d_lo) & (slot < d_hi), 1.0 / total, 0.0)
        p = jnp.concatenate([e0, e1, e2], axis=0) * inv
        p_low = p.astype(bf16)
        yield
        dv = dot_nn(p_low, gs)
        ds = (p * (dp - dots)).astype(bf16)
        yield
        dk = dot_nn(ds, qs)
        dq = gather_heads(dot_tn(ds, keys))
        yield
        for which, (ref, ext, part) in enumerate(((dk_buf, dke_ref, dk), (dv_buf, dve_ref, dv))):
            first = part[:edge]
            if i > 0:
                first = first + held[(i - 1, which)]
                ref[k0 : k0 + edge, cols] = first.astype(bf16)
            else:
                ext[:edge, cols] = first.astype(bf16)
            ref[k0 + edge : k0 + gk, cols] = part[edge:gk].astype(bf16)
            if i < n_ex - 2:
                held[(i, which)] = part[gk:]
            else:
                ext[edge:, cols] = part[gk:].astype(bf16)
        first = dq[:gq]
        if i > 0:
            dq_buf[q0 : q0 + gq, cols] = (first + held[(i - 1, 2)]).astype(bf16)
        else:
            dqe_ref[:gq, cols] = first.astype(bf16)
        if i < n_ex - 2:
            held[(i, 2)] = dq[gq:]
        else:
            dqe_ref[gq:, cols] = dq[gq:].astype(bf16)
        yield

    def copies(at):
        cols = pl.ds(pl.multiple_of(at * (BATCH * LANES), LANES), BATCH * LANES)
        out = []
        k_rows, q_rows = pl.ds(edge, (n_ex - 1) * gk - edge), pl.ds(gq, (n_ex - 2) * gq)
        for j, (buf, ref, rows) in enumerate(((dk_buf, dk_out, k_rows), (dv_buf, dv_out, k_rows), (dq_buf, dq_out, q_rows))):
            out.append(pltpu.make_async_copy(buf.at[rows, cols], ref.at[rows, cols], sems.at[at, j]))
        return out

    @pl.loop(0, q_ref.shape[1] // LANES // BATCH)
    def _(at):
        units = []
        for c in range(BATCH):
            cols = pl.ds(pl.multiple_of(at * (BATCH * LANES) + c * LANES, LANES), LANES)
            held = {}
            units += [unit(i, cols, held) for i in range(n_ex - 1)]
        run_skewed(units)
        for copy in copies(at):
            copy.start()

    @pl.loop(0, q_ref.shape[1] // LANES // BATCH)
    def _(at):
        for copy in copies(at):
            copy.wait()


def three_parts(x):
    hi = x.astype(jnp.bfloat16).astype(jnp.float32)
    mid = (x - hi).astype(jnp.bfloat16).astype(jnp.float32)
    return [hi, mid, x - hi - mid]


def as_rows(parts):
    row = lax.broadcasted_iota(jnp.int32, (8, LANES), 0)
    out = jnp.zeros((8, LANES), jnp.float32)
    for i, part in enumerate(parts):
        out = jnp.where(row == i, part, out)
    return out.astype(jnp.bfloat16)


def stats_kernel(shape, pos_ref, dec_hbm, enc_hbm, q_hbm, o_hbm, g_hbm, k_hbm, me_ref, mo_ref, stat_ref, q_ref, o_ref, g_ref, k_ref, dec_ref, enc_ref, sems):
    bounds = Bounds(shape, (dec_ref, enc_ref, pos_ref))
    n_ex, gq, gk = bounds.n_ex, bounds.gq, bounds.gk
    edge = gk // 2
    last = (n_ex - 1) * gq
    at_e = pl.multiple_of(jnp.where(bounds.even, last, 0), gq)
    at_o = pl.multiple_of(jnp.where(bounds.even, 0, last), gq)

    jobs = [
        (dec_hbm, dec_ref, None, None), (enc_hbm, enc_ref, None, None),
        (k_hbm, k_ref, (n_ex - 1) * gk, (0, gk)), (k_hbm, k_ref, 0, (gk, edge)),
    ]
    for src, dst in ((q_hbm, q_ref), (g_hbm, g_ref), (o_hbm, o_ref)):
        jobs += [(src, dst, last, (last, gq)), (src, dst, 0, (0, gq))]
    first = len(jobs)
    jobs += [(q_hbm, me_ref, at_e, (0, gq)), (g_hbm, me_ref, at_e, (gq, gq)), (q_hbm, mo_ref, at_o, (0, gq)), (g_hbm, mo_ref, at_o, (gq, gq))]
    jobs += [(src, dst, gq, (gq, last - gq)) for src, dst in ((q_hbm, q_ref), (g_hbm, g_ref), (o_hbm, o_ref))]
    copies = []
    for i, (src, dst, at, to) in enumerate(jobs):
        if to is not None:
            src, dst = src.at[pl.ds(at, to[1])], dst.at[pl.ds(*to)]
        copies.append(pltpu.make_async_copy(src, dst, sems.at[i]))
    for copy in copies:
        copy.start()
    for copy in copies[:first]:
        copy.wait()

    def both(ref, cols):
        return jnp.concatenate([ref[last:, cols], ref[:gq, cols]], axis=0)

    def unit(cols):
        qs = spread(both(q_ref, cols))
        s = dot_nt(k_ref[:, cols], qs)
        yield
        dots = row_dots(both(o_ref, cols), spread(both(g_ref, cols)))
        yield
        top, _, _, _, total = exp_sum(*edge_mask(bounds, s, False))
        logs = top + jnp.log(total)
        stat_ref[0:1, cols] = logs
        stat_ref[1:2, cols] = dots
        rows = as_rows(three_parts(logs) + three_parts(dots))
        me_ref[2 * gq :, cols] = rows
        mo_ref[2 * gq :, cols] = rows
        yield

    each_group(q_ref.shape[1] // LANES, 4, lambda cols: [unit(cols)])
    for copy in copies[first:]:
        copy.wait()


def pick(flag, a, b):
    return jnp.where(flag, a, b)


def edge_rows(ref, cols, gk):
    return jnp.concatenate([ref[ref.shape[0] - gk :, cols], ref[: gk // 2, cols]], axis=0)


def remote_kernel(shape, *refs):
    *table, _, re_ref, ro_ref, k_ref, v_ref, me_ref, mo_ref, p_ref, ds_ref = refs
    bounds = Bounds(shape, table)
    gq, gk = bounds.gq, bounds.gk
    even = bounds.even
    slot = slot_of(2 * gq)
    bf16, f32 = jnp.bfloat16, jnp.float32

    def unit(cols):
        re, ro = re_ref[: 2 * gq, cols], ro_ref[: 2 * gq, cols]
        before, after = pick(even, ro, re), pick(even, re, ro)
        qs = spread(jnp.concatenate([before[:gq], after[:gq]], axis=0))
        keys = edge_rows(k_ref, cols, gk)
        s = dot_nt(keys, qs)
        gs = spread(jnp.concatenate([before[gq:], after[gq:]], axis=0))
        dp = dot_nt(edge_rows(v_ref, cols, gk), gs)
        yield
        te, to = re_ref[2 * gq :, cols].astype(f32), ro_ref[2 * gq :, cols].astype(f32)
        tbefore, tafter = pick(even, to, te), pick(even, te, to)
        stat = jnp.where(slot < gq, tbefore, tafter)
        top, e0, e1, e2, total = exp_sum(*edge_mask(bounds, s, True))
        mine = top + jnp.log(total)
        yield
        whole = log_add(mine, stat[0:1] + stat[1:2] + stat[2:3])
        dots = stat[3:4] + stat[4:5] + stat[5:6]
        scale = jnp.where(bounds.far_lanes(slot), jnp.exp(top - whole), 0.0)
        p = jnp.concatenate([e0, e1, e2], axis=0) * scale
        ds = (p * (dp - dots)).astype(bf16)
        p_ref[:, cols] = p.astype(bf16)
        ds_ref[:, cols] = ds
        yield
        dq = gather_heads(dot_tn(ds, keys)).astype(bf16)
        logs = as_rows(three_parts(mine))
        yield
        me_ref[:gq, cols] = pick(even, dq[gq:], dq[:gq])
        mo_ref[:gq, cols] = pick(even, dq[:gq], dq[gq:])
        me_ref[gq:, cols] = logs
        mo_ref[gq:, cols] = logs
        yield

    each_group(re_ref.shape[1] // LANES, 4, lambda cols: [unit(cols)])


def ready_kernel(shape, *refs):
    *table, re_ref, ro_ref, own_ref, q_ref, g_ref, k_ref, v_ref, p_far, ds_far, dke_ref, dve_ref, p_ref, ds_ref, dk_ref, dv_ref = refs
    bounds = Bounds(shape, table)
    gq, gk = bounds.gq, bounds.gk
    edge = gk // 2
    even = bounds.even
    slot = slot_of(2 * gq)
    f32 = jnp.float32

    def far_unit(cols):
        re, ro = re_ref[: 2 * gq, cols], ro_ref[: 2 * gq, cols]
        before, after = pick(even, ro, re), pick(even, re, ro)
        gs = spread(jnp.concatenate([before[gq:], after[gq:]], axis=0))
        dv = dot_nn(p_far[:, cols], gs)
        yield
        qs = spread(jnp.concatenate([before[:gq], after[:gq]], axis=0))
        dk = dot_nn(ds_far[:, cols], qs)
        yield
        for ref, ext, part in ((dv_ref, dve_ref, dv), (dk_ref, dke_ref, dk)):
            ref[:edge, cols] = part[:edge] + ext[edge:, cols].astype(f32)
            ref[edge:gk, cols] = part[edge:gk]
            ref[gk:, cols] = part[gk:] + ext[:edge, cols].astype(f32)
        yield

    def own_unit(cols):
        qs = spread(both(q_ref, cols))
        s = dot_nt(edge_rows(k_ref, cols, gk), qs)
        gs = spread(both(g_ref, cols))
        dp = dot_nt(edge_rows(v_ref, cols, gk), gs)
        yield
        logs = jnp.where(bounds.own_lanes(slot), own_ref[0:1, cols], high)
        p = jnp.exp(jnp.concatenate(edge_mask(bounds, s, False), axis=0) - logs)
        p_ref[:, cols] = p
        yield
        ds_ref[:, cols] = p * (dp - own_ref[1:2, cols])
        yield

    def both(ref, cols):
        return jnp.concatenate([ref[ref.shape[0] - gq :, cols], ref[:gq, cols]], axis=0)

    each_group(re_ref.shape[1] // LANES, 4, lambda cols: [own_unit(cols), far_unit(cols)])


def edge_kernel(shape, *refs):
    *table, me_ref, mo_ref, own_ref, q_ref, g_ref, k_ref, p_ref, ds_ref, dka_ref, dva_ref, dqe_ref = refs[:14]
    _, _, _, dq_out, dk_out, dv_out, dq_buf, dk_buf, dv_buf, sems = refs[14:]
    bounds = Bounds(shape, table)
    n_ex, gq, gk = bounds.n_ex, bounds.gq, bounds.gk
    edge = gk // 2
    even = bounds.even
    slot = slot_of(2 * gq)
    bf16, f32 = jnp.bfloat16, jnp.float32
    last_q, last_k = (n_ex - 1) * gq, (n_ex - 1) * gk

    def both(ref, cols):
        return jnp.concatenate([ref[last_q:, cols], ref[:gq, cols]], axis=0)

    def unit(cols):
        me, mo = me_ref[gq:, cols].astype(f32), mo_ref[gq:, cols].astype(f32)
        before, after = pick(even, mo, me), pick(even, me, mo)
        before = before[0:1] + before[1:2] + before[2:3]
        after = jnp.where(bounds.has_next, after[0:1] + after[1:2] + after[2:3], low)
        own = own_ref[0:1, cols]
        share = jnp.exp(own - log_add(own, jnp.where(slot < gq, after, before)))
        share = jnp.where(bounds.own_lanes(slot), share, 0.0)
        gs = spread(both(g_ref, cols))
        dv = dot_nn((p_ref[:, cols] * share).astype(bf16), gs)
        yield
        qs = spread(both(q_ref, cols))
        ds = (ds_ref[:, cols] * share).astype(bf16)
        dk = dot_nn(ds, qs)
        yield
        dq = gather_heads(dot_tn(ds, edge_rows(k_ref, cols, gk)))
        yield
        dv_buf[:, cols] = (dv + dva_ref[:, cols]).astype(bf16)
        dk_buf[:, cols] = (dk + dka_ref[:, cols]).astype(bf16)
        me, mo = me_ref[:gq, cols].astype(f32), mo_ref[:gq, cols].astype(f32)
        before, after = pick(even, mo, me), pick(even, me, mo)
        dq_buf[:gq, cols] = (dq[gq:] + before + dqe_ref[:gq, cols].astype(f32)).astype(bf16)
        dq_buf[gq:, cols] = (dq[:gq] + after + dqe_ref[gq:, cols].astype(f32)).astype(bf16)
        yield

    def copies(at):
        cols = pl.ds(pl.multiple_of(at * (BATCH * LANES), LANES), BATCH * LANES)
        moves = []
        for buf, ref in ((dk_buf, dk_out), (dv_buf, dv_out)):
            moves += [(buf, (0, gk), ref, (last_k, gk)), (buf, (gk, edge), ref, (0, edge))]
        moves += [(dq_buf, (0, gq), dq_out, (0, gq)), (dq_buf, (gq, gq), dq_out, (last_q, gq))]
        return [
            pltpu.make_async_copy(src.at[pl.ds(*a), cols], dst.at[pl.ds(*b), cols], sems.at[at, j])
            for j, (src, a, dst, b) in enumerate(moves)
        ]

    turns = q_ref.shape[1] // LANES // BATCH

    @pl.loop(0, turns)
    def _(at):
        units = []
        for c in range(BATCH):
            units.append(unit(pl.ds(pl.multiple_of(at * (BATCH * LANES) + c * LANES, LANES), LANES)))
        run_skewed(units)
        for copy in copies(at):
            copy.start()

    @pl.loop(0, turns)
    def _(at):
        for copy in copies(at):
            copy.wait()


inside = pl.BlockSpec(memory_space=pltpu.VMEM)
anywhere = pl.BlockSpec(memory_space=pl.ANY)
off_chip = pl.BlockSpec(memory_space=pltpu.HBM)
scalars = pl.BlockSpec(memory_space=pltpu.SMEM)


def call(kernel, ins, outs, scratch=(), aliases=None, flops=0, nbytes=0):
    return pl.pallas_call(
        kernel,
        out_shape=[shape for _, shape in outs],
        in_specs=list(ins),
        out_specs=[spec for spec, _ in outs],
        scratch_shapes=list(scratch),
        input_output_aliases=aliases or {},
        compiler_params=pltpu.CompilerParams(vmem_limit_bytes=40 * 1024 * 1024),
        cost_estimate=pl.CostEstimate(flops=flops, bytes_accessed=nbytes, transcendentals=0),
    )


def shards(dec_query, enc_key, enc_value, saved_out, d_out, dec_start, enc_start):
    q, k, v, o, g = dec_query[0], enc_key[0], enc_value[0], saved_out[0], d_out[0]
    q_rows, feats = q.shape
    k_rows = k.shape[0]
    pos = lax.axis_index("seq")
    count = lax.axis_size("seq")
    n_ex = (dec_start.shape[1] - 1) // count
    gq, gk = q_rows // n_ex, k_rows // n_ex
    edge = gk // 2
    groups = feats // LANES
    bf16, f32 = jnp.bfloat16, jnp.float32
    shape = (n_ex, gq, gk, count)

    def swap_even(x):
        return lax.ppermute(x, "seq", [(i, i ^ 1) for i in range(count) if i ^ 1 < count])

    def swap_odd(x):
        pairs = []
        for i in range(1, count - 1, 2):
            pairs += [(i, i + 1), (i + 1, i)]
        return lax.ppermute(x, "seq", pairs)

    place = pos.astype(jnp.int32)[None]
    table = (dec_start, enc_start, place)
    tables = [scalars] * 3

    def like(rows, kind=bf16):
        return jax.ShapeDtypeStruct((rows, feats), kind)

    def vmem(rows):
        return pltpu.VMEM((rows, feats), bf16)

    def out(rows, kind=bf16):
        return (inside, like(rows, kind))

    placed = (pltpu.with_memory_space_constraint(x, pltpu.HBM) for x in (dec_start, enc_start, q, o, g, k))
    raw_e, raw_o, own, q, o, g = call(
        functools.partial(stats_kernel, shape), [scalars] + [off_chip] * 6,
        [out(2 * gq + 8)] * 2 + [out(2, f32)] + [out(q_rows)] * 3,
        scratch=[vmem(gk + edge), pltpu.SMEM(dec_start.shape, jnp.int32), pltpu.SMEM(enc_start.shape, jnp.int32), pltpu.SemaphoreType.DMA((17,))],
        flops=int(4e8), nbytes=int(2e6),
    )(place, *placed)
    raw_e, raw_o = swap_even(raw_e), swap_odd(raw_o)

    big = [(anywhere, like(q_rows)), (anywhere, like(k_rows)), (anywhere, like(k_rows))]
    dq, dk, dv, dqe, dke, dve = call(
        functools.partial(interior_kernel, shape), tables + [anywhere] + [inside] * 5,
        big + [out(2 * gq), out(gk), out(gk)],
        scratch=[vmem(q_rows), vmem(k_rows), vmem(k_rows), pltpu.SemaphoreType.DMA((groups // BATCH, 3))],
        flops=int(4e9), nbytes=int(8e6),
    )(*table, own, q, o, g, k, v)

    to_e, to_o, p_far, ds_far = call(
        functools.partial(remote_kernel, shape), tables + [anywhere] + [inside] * 4,
        [out(gq + 8)] * 2 + [out(gk + edge)] * 2,
        flops=int(8e8), nbytes=int(3e6),
    )(*table, dqe, raw_e, raw_o, k, v)
    back_e, back_o = swap_even(to_e), swap_odd(to_o)

    p_own, ds_own, dka, dva = call(
        functools.partial(ready_kernel, shape), tables + [inside] * 11, [out(gk + edge, f32)] * 4,
        flops=int(1e9), nbytes=int(6e6),
    )(*table, raw_e, raw_o, own, q, g, k, v, p_far, ds_far, dke, dve)
    dq, dk, dv = call(
        functools.partial(edge_kernel, shape), tables + [inside] * 11 + [anywhere] * 3, big,
        scratch=[vmem(2 * gq), vmem(gk + edge), vmem(gk + edge), pltpu.SemaphoreType.DMA((groups // BATCH, 6))],
        aliases={14: 0, 15: 1, 16: 2},
        flops=int(1e9), nbytes=int(6e6),
    )(*table, back_e, back_o, own, q, g, k, p_own, ds_own, dka, dva, dqe, dq, dk, dv)
    return dq[None], dk[None], dv[None]


def solution(mesh):
    spec = P(("grp", "dp"), "seq", None)
    return jax.shard_map(
        shards,
        mesh=mesh,
        in_specs=(spec,) * 5 + (P(("grp", "dp"), None),) * 2,
        out_specs=(spec,) * 3,
        check_vma=False,
    )
```

```python
import functools

import jax
import jax.numpy as jnp
from jax import lax
from jax.experimental import pallas as pl
from jax.experimental.pallas import tpu as pltpu
from jax.sharding import PartitionSpec as P

H = 32
HD = 64
LANES = 256
PER = LANES // HD

low = -1e30
high = 1e30
BATCH = 4


def dot_nt(a, b):
    return lax.dot_general(a, b, (((1,), (1,)), ((), ())), preferred_element_type=jnp.float32)


def dot_nn(a, b):
    return lax.dot_general(a, b, (((1,), (0,)), ((), ())), preferred_element_type=jnp.float32)


def dot_tn(a, b):
    return lax.dot_general(a, b, (((0,), (0,)), ((), ())), preferred_element_type=jnp.float32)


def spread(rows):
    half = LANES // 2
    side = lax.broadcasted_iota(jnp.int32, (rows.shape[0], half), 1) // HD
    empty = jnp.zeros((rows.shape[0], half), rows.dtype)
    out = []
    for h in range(PER):
        at, within = divmod(h * HD, half)
        piece = jnp.where(side == within // HD, rows[:, at * half : (at + 1) * half], empty)
        out.append(jnp.concatenate([piece if at == x else empty for x in range(LANES // half)], axis=1))
    return jnp.concatenate(out, axis=0)


def gather_heads(full):
    slots, half = full.shape[0] // PER, LANES // 2
    side = lax.broadcasted_iota(jnp.int32, (slots, half), 1) // HD
    out = []
    for at in range(LANES // half):
        lanes = slice(at * half, (at + 1) * half)
        heads = [h for h in range(PER) if h * HD // half == at]
        part = full[heads[0] * slots : (heads[0] + 1) * slots, lanes]
        for n, h in enumerate(heads[1:], 1):
            part = jnp.where(side == n, full[h * slots : (h + 1) * slots, lanes], part)
        out.append(part)
    return jnp.concatenate(out, axis=1)


def slot_of(slots):
    return lax.rem(lax.broadcasted_iota(jnp.int32, (1, PER * slots), 1), slots)


def row_dots(outs, spread_grads):
    slots = outs.shape[0]
    full = dot_nt(outs, spread_grads)
    row = lax.broadcasted_iota(jnp.int32, full.shape, 0)
    lane = lax.rem(lax.broadcasted_iota(jnp.int32, full.shape, 1), slots)
    return jnp.sum(jnp.where(row == lane, full, 0.0), axis=0, keepdims=True)


def log_add(a, b):
    top = jnp.maximum(a, b)
    return top + jnp.log(jnp.exp(a - top) + jnp.exp(b - top))


def row_ids(rows, lanes):
    return lax.broadcasted_iota(jnp.int32, (rows, lanes), 0)


def run_skewed(units):
    live, queue = [], list(units)
    while queue or live:
        if queue:
            live.append(queue.pop(0))
        for unit in list(live):
            try:
                next(unit)
            except StopIteration:
                live.remove(unit)


def each_group(groups, batch, units_of, after=None):
    @pl.loop(0, groups // batch)
    def _(at):
        units = []
        for c in range(batch):
            units += units_of(Group(at * batch, c))
        run_skewed(units)
        if after is not None:
            after(at)


class Group:
    def __init__(self, base, c):
        self.base, self.c = base, c
        self.cols = self.lanes(LANES)

    def lanes(self, width):
        return pl.ds(pl.multiple_of(self.base * width + self.c * width, width), width)

    def row(self, per, i):
        return pl.ds(pl.multiple_of(self.base * per, per) + (self.c * per + i), 1)


class Bounds:
    def __init__(self, shape, table):
        self.n_ex, self.gq, self.gk, self.count = shape
        self.dec_ref, self.enc_ref, pos_ref = table
        self.pos = pos_ref[0]
        self.even = lax.rem(self.pos, 2) == 0
        self.has_next = self.pos < self.count - 1

    def dec(self, i):
        return self.dec_ref[0, self.pos * self.n_ex + i] - self.pos * (self.n_ex * self.gq)

    def enc(self, i):
        return self.enc_ref[0, self.pos * self.n_ex + i] - self.pos * (self.n_ex * self.gk)

    def prior(self):
        at = jnp.maximum(self.pos * self.n_ex - 1, 0)
        rows = self.dec_ref[0, at] - self.pos * (self.n_ex * self.gq) + self.gq
        return jnp.where(self.pos > 0, rows, self.gq)

    def far_lanes(self, side, slot):
        return slot < self.dec(self.n_ex) - self.n_ex * self.gq if side == 0 else slot >= self.prior()

    def own_lanes(self, side, slot):
        return slot >= self.dec(self.n_ex - 1) - (self.n_ex - 1) * self.gq if side == 0 else slot < self.dec(0)

    def edge_mask(self, side, s):
        edge = self.gk // 2
        row = row_ids(edge, s.shape[1])
        if side == 1:
            return jnp.where(row < self.enc(0), s, low)
        first = self.enc(self.n_ex - 1) - (self.n_ex - 1) * self.gk
        return jnp.concatenate([jnp.where(row >= first, s[:edge], low), s[edge:]], axis=0)

    def edge_rows(self, side, ref, cols):
        return ref[ref.shape[0] - self.gk :, cols] if side == 0 else ref[: self.gk // 2, cols]

    def own_rows(self, side, ref, cols):
        return ref[ref.shape[0] - self.gq :, cols] if side == 0 else ref[: self.gq, cols]

    def part(self, side):
        return slice(0, self.gk) if side == 0 else slice(self.gk, self.gk + self.gk // 2)

    def from_side(self, side, even_ref, odd_ref, at):
        e, o = even_ref[at], odd_ref[at]
        return jnp.where(self.even, e, o) if side == 0 else jnp.where(self.even, o, e)


def exp_sum(s0, s1, s2):
    top = jnp.max(jnp.maximum(jnp.maximum(s0, s1), s2), axis=0, keepdims=True)
    e0, e1, e2 = jnp.exp(s0 - top), jnp.exp(s1 - top), jnp.exp(s2 - top)
    return top, e0, e1, e2, jnp.sum(e0 + e1 + e2, axis=0, keepdims=True)


def exp_top(s):
    top = jnp.max(s, axis=0, keepdims=True)
    e = jnp.exp(s - top)
    return top, e, jnp.sum(e, axis=0, keepdims=True)


def interior_kernel(shape, *refs):
    table, (_, q_ref, o_ref, g_ref, k_ref, v_ref), refs = refs[:3], refs[3:9], refs[9:]
    dq_out, dk_out, dv_out, dqe_ref, dke_ref, dve_ref, dq_buf, dk_buf, dv_buf, sems = refs
    bounds = Bounds(shape, table)
    n_ex, gq, gk = bounds.n_ex, bounds.gq, bounds.gk
    slots = 2 * gq
    edge = gk // 2
    win = gk + edge
    slot = slot_of(slots)
    bf16 = jnp.bfloat16

    def unit(i, cols, held):
        q0, k0 = i * gq, i * gk
        d_lo, d_hi = bounds.dec(i) - q0, bounds.dec(i + 1) - q0
        e_lo, e_hi = bounds.enc(i) - k0, bounds.enc(i + 1) - k0 - gk
        keys = k_ref[k0 : k0 + win, cols]
        qs = spread(q_ref[q0 : q0 + slots, cols])
        s = dot_nt(keys, qs)
        gs = spread(g_ref[q0 : q0 + slots, cols])
        dots = row_dots(o_ref[q0 : q0 + slots, cols], gs)
        dp = dot_nt(v_ref[k0 : k0 + win, cols], gs)
        yield
        row = row_ids(edge, LANES)
        s0 = jnp.where(row >= e_lo, s[:edge], low)
        s2 = jnp.where(row < e_hi, s[gk:], low)
        _, e0, e1, e2, total = exp_sum(s0, s[edge:gk], s2)
        yield
        inv = jnp.where((slot >= d_lo) & (slot < d_hi), 1.0 / total, 0.0)
        p = jnp.concatenate([e0, e1, e2], axis=0) * inv
        p_low = p.astype(bf16)
        yield
        dv = dot_nn(p_low, gs)
        ds = (p * (dp - dots)).astype(bf16)
        yield
        dk = dot_nn(ds, qs)
        dq = gather_heads(dot_tn(ds, keys))
        yield
        for which, (ref, ext, part) in enumerate(((dk_buf, dke_ref, dk), (dv_buf, dve_ref, dv))):
            first = part[:edge]
            if i > 0:
                first = first + held[(i - 1, which)]
                ref[k0 : k0 + edge, cols] = first.astype(bf16)
            else:
                ext[:edge, cols] = first.astype(bf16)
            ref[k0 + edge : k0 + gk, cols] = part[edge:gk].astype(bf16)
            if i < n_ex - 2:
                held[(i, which)] = part[gk:]
            else:
                ext[edge:, cols] = part[gk:].astype(bf16)
        first = dq[:gq]
        if i > 0:
            dq_buf[q0 : q0 + gq, cols] = (first + held[(i - 1, 2)]).astype(bf16)
        else:
            dqe_ref[:gq, cols] = first.astype(bf16)
        if i < n_ex - 2:
            held[(i, 2)] = dq[gq:]
        else:
            dqe_ref[gq:, cols] = dq[gq:].astype(bf16)
        yield

    def copies(at):
        cols = pl.ds(pl.multiple_of(at * (BATCH * LANES), LANES), BATCH * LANES)
        out = []
        k_rows, q_rows = pl.ds(edge, (n_ex - 1) * gk - edge), pl.ds(gq, (n_ex - 2) * gq)
        for j, (buf, ref, rows) in enumerate(((dk_buf, dk_out, k_rows), (dv_buf, dv_out, k_rows), (dq_buf, dq_out, q_rows))):
            out.append(pltpu.make_async_copy(buf.at[rows, cols], ref.at[rows, cols], sems.at[at, j]))
        return out

    @pl.loop(0, q_ref.shape[1] // LANES // BATCH)
    def _(at):
        units = []
        for c in range(BATCH):
            cols = pl.ds(pl.multiple_of(at * (BATCH * LANES) + c * LANES, LANES), LANES)
            held = {}
            units += [unit(i, cols, held) for i in range(n_ex - 1)]
        run_skewed(units)
        for copy in copies(at):
            copy.start()

    @pl.loop(0, q_ref.shape[1] // LANES // BATCH)
    def _(at):
        for copy in copies(at):
            copy.wait()


def three_parts(x):
    hi = x.astype(jnp.bfloat16).astype(jnp.float32)
    mid = (x - hi).astype(jnp.bfloat16).astype(jnp.float32)
    return [hi, mid, x - hi - mid]


def stats_kernel(shape, pos_ref, dec_hbm, enc_hbm, q_hbm, o_hbm, g_hbm, k_hbm, me_ref, mo_ref, stat_ref, q_ref, o_ref, g_ref, k_ref, pack_ref, dec_ref, enc_ref, sems):
    bounds = Bounds(shape, (dec_ref, enc_ref, pos_ref))
    n_ex, gq, gk = bounds.n_ex, bounds.gq, bounds.gk
    edge = gk // 2
    last = (n_ex - 1) * gq
    feats = q_ref.shape[1]
    at_e = pl.multiple_of(jnp.where(bounds.even, last, 0), gq)
    at_o = pl.multiple_of(jnp.where(bounds.even, 0, last), gq)

    jobs = [
        (dec_hbm, dec_ref, None, None), (enc_hbm, enc_ref, None, None),
        (k_hbm, k_ref, (n_ex - 1) * gk, (0, gk)), (k_hbm, k_ref, 0, (gk, edge)),
    ]
    for src, dst in ((q_hbm, q_ref), (g_hbm, g_ref), (o_hbm, o_ref)):
        jobs += [(src, dst, last, (last, gq)), (src, dst, 0, (0, gq))]
    first = len(jobs)
    jobs += [(q_hbm, me_ref, at_e, (0, gq)), (g_hbm, me_ref, at_e, (gq, gq)), (q_hbm, mo_ref, at_o, (0, gq)), (g_hbm, mo_ref, at_o, (gq, gq))]
    jobs += [(src, dst, gq, (gq, last - gq)) for src, dst in ((q_hbm, q_ref), (g_hbm, g_ref), (o_hbm, o_ref))]
    copies = []
    for i, (src, dst, at, to) in enumerate(jobs):
        if to is not None:
            src, dst = src.at[pl.ds(at, to[1])], dst.at[pl.ds(*to), pl.ds(0, feats)]
        copies.append(pltpu.make_async_copy(src, dst, sems.at[i]))
    for copy in copies:
        copy.start()
    for copy in copies[:first]:
        copy.wait()

    slots = PER * gq
    per = 2 * gq * LANES // feats

    def unit(group):
        cols = group.cols
        s, dots = [], []
        for side in (0, 1):
            keys = k_ref[bounds.part(side), cols]
            s.append(dot_nt(keys, spread(bounds.own_rows(side, q_ref, cols))))
        yield
        for side in (0, 1):
            gs = spread(bounds.own_rows(side, g_ref, cols))
            dots.append(row_dots(bounds.own_rows(side, o_ref, cols), gs))
        yield
        for side in (0, 1):
            top, _, total = exp_top(bounds.edge_mask(side, s[side]))
            logs = top + jnp.log(total)
            stat_ref[2 * side : 2 * side + 1, group.lanes(slots)] = logs
            stat_ref[2 * side + 1 : 2 * side + 2, group.lanes(slots)] = dots[side]
            for i, part in enumerate(three_parts(logs) + three_parts(dots[side])):
                pack_ref[side, group.row(per, i), :] = part
        yield

    each_group(feats // LANES, BATCH, lambda group: [unit(group)])
    for copy in copies[first:]:
        copy.wait()
    after, before = pack_ref[0].astype(jnp.bfloat16), pack_ref[1].astype(jnp.bfloat16)
    me_ref[:, feats:] = jnp.where(bounds.even, after, before)
    mo_ref[:, feats:] = jnp.where(bounds.even, before, after)


def unpack(ref, group, per, i):
    return ref[group.row(per, i), :] + ref[group.row(per, i + 1), :] + ref[group.row(per, i + 2), :]


def remote_kernel(shape, *refs):
    *table, _, re_ref, ro_ref, k_ref, v_ref, me_ref, mo_ref, p_ref, ds_ref, got_ref, pack_ref = refs
    bounds = Bounds(shape, table)
    gq, gk = bounds.gq, bounds.gk
    even = bounds.even
    feats = k_ref.shape[1]
    slots = PER * gq
    slot = slot_of(gq)
    bf16, f32 = jnp.bfloat16, jnp.float32
    per_in, per_out = 2 * gq * LANES // feats, gq * LANES // feats
    extra = (slice(None), slice(feats, None))
    for side in (0, 1):
        got_ref[side] = bounds.from_side(side, re_ref, ro_ref, extra).astype(f32)
    pack_ref[...] = jnp.zeros_like(pack_ref)

    def unit(group):
        cols = group.cols
        work = []
        for side in (0, 1):
            far = bounds.from_side(side, re_ref, ro_ref, (slice(None), cols))
            keys = bounds.edge_rows(side, k_ref, cols)
            s = dot_nt(keys, spread(far[:gq]))
            dp = dot_nt(bounds.edge_rows(side, v_ref, cols), spread(far[gq:]))
            work.append((keys, s, dp))
        yield
        tops = [exp_top(bounds.edge_mask(side, work[side][1])) for side in (0, 1)]
        yield
        ds = []
        for side in (0, 1):
            top, e, total = tops[side]
            mine = top + jnp.log(total)
            whole = log_add(mine, unpack(got_ref.at[side], group, per_in, 0))
            dots = unpack(got_ref.at[side], group, per_in, 3)
            p = e * jnp.where(bounds.far_lanes(side, slot), jnp.exp(top - whole), 0.0)
            ds.append((p * (work[side][2] - dots)).astype(bf16))
            p_ref[bounds.part(side), group.lanes(slots)] = p.astype(bf16)
            ds_ref[bounds.part(side), group.lanes(slots)] = ds[side]
            for i, part in enumerate(three_parts(mine)):
                pack_ref[side, group.row(per_out, i), :] = part
        yield
        after, before = (gather_heads(dot_tn(ds[side], work[side][0])).astype(bf16) for side in (0, 1))
        yield
        me_ref[:, cols] = jnp.where(even, after, before)
        mo_ref[:, cols] = jnp.where(even, before, after)
        yield

    each_group(feats // LANES, BATCH, lambda group: [unit(group)])
    after, before = pack_ref[0].astype(bf16), pack_ref[1].astype(bf16)
    me_ref[:, feats:] = jnp.where(even, after, before)
    mo_ref[:, feats:] = jnp.where(even, before, after)


def ready_kernel(shape, *refs):
    *table, re_ref, ro_ref, own_ref, q_ref, g_ref, k_ref, v_ref, p_far, ds_far, dke_ref, dve_ref, p_ref, ds_ref, dk_ref, dv_ref = refs
    bounds = Bounds(shape, table)
    gq, gk = bounds.gq, bounds.gk
    edge = gk // 2
    slots = PER * gq
    slot = slot_of(gq)
    f32 = jnp.float32

    def far_unit(group):
        cols, lanes = group.cols, group.lanes(slots)
        far = [bounds.from_side(side, re_ref, ro_ref, (slice(None), cols)) for side in (0, 1)]
        for ref, ext, src, rows in ((dv_ref, dve_ref, p_far, slice(gq, None)), (dk_ref, dke_ref, ds_far, slice(0, gq))):
            a, b = (dot_nn(src[bounds.part(side), lanes], spread(far[side][rows])) for side in (0, 1))
            yield
            ref[:edge, cols] = a[:edge] + ext[edge:, cols].astype(f32)
            ref[edge:gk, cols] = a[edge:]
            ref[gk:, cols] = b + ext[:edge, cols].astype(f32)
        yield

    def own_unit(group):
        cols, lanes = group.cols, group.lanes(slots)
        work = []
        for side in (0, 1):
            s = dot_nt(bounds.edge_rows(side, k_ref, cols), spread(bounds.own_rows(side, q_ref, cols)))
            dp = dot_nt(bounds.edge_rows(side, v_ref, cols), spread(bounds.own_rows(side, g_ref, cols)))
            work.append((s, dp))
        yield
        for side in (0, 1):
            s, dp = work[side]
            logs = jnp.where(bounds.own_lanes(side, slot), own_ref[2 * side : 2 * side + 1, lanes], high)
            p = jnp.exp(bounds.edge_mask(side, s) - logs)
            p_ref[bounds.part(side), lanes] = p
            ds_ref[bounds.part(side), lanes] = p * (dp - own_ref[2 * side + 1 : 2 * side + 2, lanes])
        yield

    each_group(q_ref.shape[1] // LANES, 4, lambda group: [own_unit(group), far_unit(group)])


def edge_kernel(shape, *refs):
    *table, me_ref, mo_ref, own_ref, q_ref, g_ref, k_ref, p_ref, ds_ref, dka_ref, dva_ref, dqe_ref = refs[:14]
    _, _, _, dq_out, dk_out, dv_out, dq_buf, dk_buf, dv_buf, got_ref, sems = refs[14:]
    bounds = Bounds(shape, table)
    n_ex, gq, gk = bounds.n_ex, bounds.gq, bounds.gk
    edge = gk // 2
    feats = q_ref.shape[1]
    slots = PER * gq
    slot = slot_of(gq)
    bf16, f32 = jnp.bfloat16, jnp.float32
    last_q, last_k = (n_ex - 1) * gq, (n_ex - 1) * gk
    per = gq * LANES // feats
    extra = (slice(None), slice(feats, None))
    for side in (0, 1):
        got_ref[side] = bounds.from_side(side, me_ref, mo_ref, extra).astype(f32)

    def unit(group):
        cols, lanes = group.cols, group.lanes(slots)
        shares = []
        for side in (0, 1):
            other = unpack(got_ref.at[side], group, per, 0)
            if side == 0:
                other = jnp.where(bounds.has_next, other, low)
            own = own_ref[2 * side : 2 * side + 1, lanes]
            share = jnp.where(bounds.own_lanes(side, slot), jnp.exp(own - log_add(own, other)), 0.0)
            shares.append(share)
            part = bounds.part(side)
            dv = dot_nn((p_ref[part, lanes] * share).astype(bf16), spread(bounds.own_rows(side, g_ref, cols)))
            dv_buf[part, cols] = (dv + dva_ref[part, cols]).astype(bf16)
        yield
        ds = []
        for side in (0, 1):
            part = bounds.part(side)
            ds.append((ds_ref[part, lanes] * shares[side]).astype(bf16))
            dk = dot_nn(ds[side], spread(bounds.own_rows(side, q_ref, cols)))
            dk_buf[part, cols] = (dk + dka_ref[part, cols]).astype(bf16)
        yield
        for side in (0, 1):
            dq = gather_heads(dot_tn(ds[side], bounds.edge_rows(side, k_ref, cols)))
            back = bounds.from_side(side, me_ref, mo_ref, (slice(None), cols)).astype(f32)
            rows = slice(gq, 2 * gq) if side == 0 else slice(0, gq)
            dq_buf[rows, cols] = (dq + back + dqe_ref[rows, cols].astype(f32)).astype(bf16)
        yield

    def copies(at):
        cols = pl.ds(pl.multiple_of(at * (BATCH * LANES), LANES), BATCH * LANES)
        moves = []
        for buf, ref in ((dk_buf, dk_out), (dv_buf, dv_out)):
            moves += [(buf, (0, gk), ref, (last_k, gk)), (buf, (gk, edge), ref, (0, edge))]
        moves += [(dq_buf, (0, gq), dq_out, (0, gq)), (dq_buf, (gq, gq), dq_out, (last_q, gq))]
        return [
            pltpu.make_async_copy(src.at[pl.ds(*a), cols], dst.at[pl.ds(*b), cols], sems.at[at, j])
            for j, (src, a, dst, b) in enumerate(moves)
        ]

    def send(at):
        for copy in copies(at):
            copy.start()

    each_group(feats // LANES, BATCH, lambda group: [unit(group)], send)

    @pl.loop(0, feats // LANES // BATCH)
    def _(at):
        for copy in copies(at):
            copy.wait()


inside = pl.BlockSpec(memory_space=pltpu.VMEM)
anywhere = pl.BlockSpec(memory_space=pl.ANY)
off_chip = pl.BlockSpec(memory_space=pltpu.HBM)
scalars = pl.BlockSpec(memory_space=pltpu.SMEM)


def call(kernel, ins, outs, scratch=(), aliases=None, flops=0, nbytes=0):
    return pl.pallas_call(
        kernel,
        out_shape=[shape for _, shape in outs],
        in_specs=list(ins),
        out_specs=[spec for spec, _ in outs],
        scratch_shapes=list(scratch),
        input_output_aliases=aliases or {},
        compiler_params=pltpu.CompilerParams(vmem_limit_bytes=40 * 1024 * 1024),
        cost_estimate=pl.CostEstimate(flops=flops, bytes_accessed=nbytes, transcendentals=0),
    )


def shards(dec_query, enc_key, enc_value, saved_out, d_out, dec_start, enc_start):
    q, k, v, o, g = dec_query[0], enc_key[0], enc_value[0], saved_out[0], d_out[0]
    q_rows, feats = q.shape
    k_rows = k.shape[0]
    pos = lax.axis_index("seq")
    count = lax.axis_size("seq")
    n_ex = (dec_start.shape[1] - 1) // count
    gq, gk = q_rows // n_ex, k_rows // n_ex
    edge = gk // 2
    groups = feats // LANES
    bf16, f32 = jnp.bfloat16, jnp.float32
    shape = (n_ex, gq, gk, count)

    def swap_even(x):
        return lax.ppermute(x, "seq", [(i, i ^ 1) for i in range(count) if i ^ 1 < count])

    def swap_odd(x):
        pairs = []
        for i in range(1, count - 1, 2):
            pairs += [(i, i + 1), (i + 1, i)]
        return lax.ppermute(x, "seq", pairs)

    place = pos.astype(jnp.int32)[None]
    table = (dec_start, enc_start, place)
    tables = [scalars] * 3

    packed = groups * PER * gq

    def like(rows, kind=bf16, width=feats):
        return jax.ShapeDtypeStruct((rows, width), kind)

    def vmem(rows):
        return pltpu.VMEM((rows, feats), bf16)

    def out(rows, kind=bf16, width=feats):
        return (inside, like(rows, kind, width))

    def pack(rows):
        return pltpu.VMEM((2, rows, PER * gq), f32)

    placed = (pltpu.with_memory_space_constraint(x, pltpu.HBM) for x in (dec_start, enc_start, q, o, g, k))
    raw_e, raw_o, own, q, o, g = call(
        functools.partial(stats_kernel, shape), [scalars] + [off_chip] * 6,
        [out(2 * gq, bf16, feats + PER * gq)] * 2 + [out(4, f32, packed)] + [out(q_rows)] * 3,
        scratch=[vmem(gk + edge), pack(2 * gq), pltpu.SMEM(dec_start.shape, jnp.int32), pltpu.SMEM(enc_start.shape, jnp.int32), pltpu.SemaphoreType.DMA((17,))],
        flops=int(4e8), nbytes=int(2e6),
    )(place, *placed)
    raw_e, raw_o = swap_even(raw_e), swap_odd(raw_o)

    big = [(anywhere, like(q_rows)), (anywhere, like(k_rows)), (anywhere, like(k_rows))]
    dq, dk, dv, dqe, dke, dve = call(
        functools.partial(interior_kernel, shape), tables + [anywhere] + [inside] * 5,
        big + [out(2 * gq), out(gk), out(gk)],
        scratch=[vmem(q_rows), vmem(k_rows), vmem(k_rows), pltpu.SemaphoreType.DMA((groups // BATCH, 3))],
        flops=int(4e9), nbytes=int(8e6),
    )(*table, own, q, o, g, k, v)

    to_e, to_o, p_far, ds_far = call(
        functools.partial(remote_kernel, shape), tables + [anywhere] + [inside] * 4,
        [out(gq, bf16, feats + PER * gq)] * 2 + [out(gk + edge, bf16, packed)] * 2,
        scratch=[pack(2 * gq), pack(gq)],
        flops=int(8e8), nbytes=int(3e6),
    )(*table, dqe, raw_e, raw_o, k, v)
    back_e, back_o = swap_even(to_e), swap_odd(to_o)

    p_own, ds_own, dka, dva = call(
        functools.partial(ready_kernel, shape), tables + [inside] * 11, [out(gk + edge, f32, packed)] * 2 + [out(gk + edge, f32)] * 2,
        flops=int(1e9), nbytes=int(6e6),
    )(*table, raw_e, raw_o, own, q, g, k, v, p_far, ds_far, dke, dve)
    dq, dk, dv = call(
        functools.partial(edge_kernel, shape), tables + [inside] * 11 + [anywhere] * 3, big,
        scratch=[vmem(2 * gq), vmem(gk + edge), vmem(gk + edge), pack(gq), pltpu.SemaphoreType.DMA((groups // BATCH, 6))],
        aliases={14: 0, 15: 1, 16: 2},
        flops=int(1e9), nbytes=int(6e6),
    )(*table, back_e, back_o, own, q, g, k, p_own, ds_own, dka, dva, dqe, dq, dk, dv)
    return dq[None], dk[None], dv[None]


def solution(mesh):
    spec = P(("grp", "dp"), "seq", None)
    return jax.shard_map(
        shards,
        mesh=mesh,
        in_specs=(spec,) * 5 + (P(("grp", "dp"), None),) * 2,
        out_specs=(spec,) * 3,
        check_vma=False,
    )
```

```python
import functools

import jax
import jax.numpy as jnp
from jax import lax
from jax.experimental import pallas as pl
from jax.experimental.pallas import tpu as pltpu
from jax.sharding import PartitionSpec as P

H = 32
HD = 64
LANES = 256
PER = LANES // HD

low = -1e30
high = 1e30
BATCH = 4
CHUNK = 2


def dot_nt(a, b):
    return lax.dot_general(a, b, (((1,), (1,)), ((), ())), preferred_element_type=jnp.float32)


def dot_nn(a, b):
    return lax.dot_general(a, b, (((1,), (0,)), ((), ())), preferred_element_type=jnp.float32)


def dot_tn(a, b):
    return lax.dot_general(a, b, (((0,), (0,)), ((), ())), preferred_element_type=jnp.float32)


def spread(rows):
    half = LANES // 2
    side = lax.broadcasted_iota(jnp.int32, (rows.shape[0], half), 1) // HD
    empty = jnp.zeros((rows.shape[0], half), rows.dtype)
    out = []
    for h in range(PER):
        at, within = divmod(h * HD, half)
        piece = jnp.where(side == within // HD, rows[:, at * half : (at + 1) * half], empty)
        out.append(jnp.concatenate([piece if at == x else empty for x in range(LANES // half)], axis=1))
    return jnp.concatenate(out, axis=0)


def gather_heads(full):
    slots, half = full.shape[0] // PER, LANES // 2
    side = lax.broadcasted_iota(jnp.int32, (slots, half), 1) // HD
    out = []
    for at in range(LANES // half):
        lanes = slice(at * half, (at + 1) * half)
        heads = [h for h in range(PER) if h * HD // half == at]
        part = full[heads[0] * slots : (heads[0] + 1) * slots, lanes]
        for n, h in enumerate(heads[1:], 1):
            part = jnp.where(side == n, full[h * slots : (h + 1) * slots, lanes], part)
        out.append(part)
    return jnp.concatenate(out, axis=1)


def slot_of(slots):
    return lax.rem(lax.broadcasted_iota(jnp.int32, (1, PER * slots), 1), slots)


def row_dots(outs, spread_grads):
    slots = outs.shape[0]
    full = dot_nt(outs, spread_grads)
    row = lax.broadcasted_iota(jnp.int32, full.shape, 0)
    lane = lax.rem(lax.broadcasted_iota(jnp.int32, full.shape, 1), slots)
    return jnp.sum(jnp.where(row == lane, full, 0.0), axis=0, keepdims=True)


def log_add(a, b):
    top = jnp.maximum(a, b)
    return top + jnp.log(jnp.exp(a - top) + jnp.exp(b - top))


def row_ids(rows, lanes):
    return lax.broadcasted_iota(jnp.int32, (rows, lanes), 0)


def run_skewed(units):
    live, queue = [], list(units)
    while queue or live:
        if queue:
            live.append(queue.pop(0))
        for unit in list(live):
            try:
                next(unit)
            except StopIteration:
                live.remove(unit)


def each_group(groups, batch, units_of, after=None):
    @pl.loop(0, groups // batch)
    def _(at):
        units = []
        for c in range(batch):
            units += units_of(Group(at * batch, c))
        run_skewed(units)
        if after is not None:
            after(at)


class Group:
    def __init__(self, base, c):
        self.base, self.c = base, c
        self.cols = self.lanes(LANES)

    def lanes(self, width):
        return pl.ds(pl.multiple_of(self.base * width + self.c * width, width), width)

    def row(self, per, i):
        return pl.ds(pl.multiple_of(self.base * per, per) + (self.c * per + i), 1)


class Bounds:
    def __init__(self, shape, table):
        self.n_ex, self.gq, self.gk, self.count = shape
        self.dec_ref, self.enc_ref, pos_ref = table
        self.pos = pos_ref[0]
        self.even = lax.rem(self.pos, 2) == 0
        self.has_next = self.pos < self.count - 1

    def dec(self, i):
        return self.dec_ref[0, self.pos * self.n_ex + i] - self.pos * (self.n_ex * self.gq)

    def enc(self, i):
        return self.enc_ref[0, self.pos * self.n_ex + i] - self.pos * (self.n_ex * self.gk)

    def prior(self):
        at = jnp.maximum(self.pos * self.n_ex - 1, 0)
        rows = self.dec_ref[0, at] - self.pos * (self.n_ex * self.gq) + self.gq
        return jnp.where(self.pos > 0, rows, self.gq)

    def far_lanes(self, side, slot):
        return slot < self.dec(self.n_ex) - self.n_ex * self.gq if side == 0 else slot >= self.prior()

    def own_lanes(self, side, slot):
        return slot >= self.dec(self.n_ex - 1) - (self.n_ex - 1) * self.gq if side == 0 else slot < self.dec(0)

    def edge_mask(self, side, s):
        edge = self.gk // 2
        row = row_ids(edge, s.shape[1])
        if side == 1:
            return jnp.where(row < self.enc(0), s, low)
        first = self.enc(self.n_ex - 1) - (self.n_ex - 1) * self.gk
        return jnp.concatenate([jnp.where(row >= first, s[:edge], low), s[edge:]], axis=0)

    def edge_rows(self, side, ref, cols):
        return ref[ref.shape[0] - self.gk :, cols] if side == 0 else ref[: self.gk // 2, cols]

    def own_rows(self, side, ref, cols):
        return ref[ref.shape[0] - self.gq :, cols] if side == 0 else ref[: self.gq, cols]

    def part(self, side):
        return slice(0, self.gk) if side == 0 else slice(self.gk, self.gk + self.gk // 2)

    def from_side(self, side, even_ref, odd_ref, at):
        e, o = even_ref[at], odd_ref[at]
        return jnp.where(self.even, e, o) if side == 0 else jnp.where(self.even, o, e)


def exp_sum(s0, s1, s2):
    top = jnp.max(jnp.maximum(jnp.maximum(s0, s1), s2), axis=0, keepdims=True)
    e0, e1, e2 = jnp.exp(s0 - top), jnp.exp(s1 - top), jnp.exp(s2 - top)
    return top, e0, e1, e2, jnp.sum(e0 + e1 + e2, axis=0, keepdims=True)


def exp_top(s):
    top = jnp.max(s, axis=0, keepdims=True)
    e = jnp.exp(s - top)
    return top, e, jnp.sum(e, axis=0, keepdims=True)


def interior_kernel(shape, *refs):
    table, (_, q_ref, o_ref, g_ref, k_ref, v_ref), refs = refs[:3], refs[3:9], refs[9:]
    dq_out, dk_out, dv_out, dqe_ref, dke_ref, dve_ref, dq_buf, dk_buf, dv_buf, sems = refs
    bounds = Bounds(shape, table)
    n_ex, gq, gk = bounds.n_ex, bounds.gq, bounds.gk
    slots = 2 * gq
    edge = gk // 2
    win = gk + edge
    slot = slot_of(slots)
    bf16 = jnp.bfloat16

    def unit(i, cols, held):
        q0, k0 = i * gq, i * gk
        d_lo, d_hi = bounds.dec(i) - q0, bounds.dec(i + 1) - q0
        e_lo, e_hi = bounds.enc(i) - k0, bounds.enc(i + 1) - k0 - gk
        keys = k_ref[k0 : k0 + win, cols]
        qs = spread(q_ref[q0 : q0 + slots, cols])
        s = dot_nt(keys, qs)
        gs = spread(g_ref[q0 : q0 + slots, cols])
        dots = row_dots(o_ref[q0 : q0 + slots, cols], gs)
        dp = dot_nt(v_ref[k0 : k0 + win, cols], gs)
        yield
        row = row_ids(edge, LANES)
        s0 = jnp.where(row >= e_lo, s[:edge], low)
        s2 = jnp.where(row < e_hi, s[gk:], low)
        _, e0, e1, e2, total = exp_sum(s0, s[edge:gk], s2)
        yield
        inv = jnp.where((slot >= d_lo) & (slot < d_hi), 1.0 / total, 0.0)
        p = jnp.concatenate([e0, e1, e2], axis=0) * inv
        p_low = p.astype(bf16)
        yield
        dv = dot_nn(p_low, gs)
        ds = (p * (dp - dots)).astype(bf16)
        yield
        dk = dot_nn(ds, qs)
        dq = gather_heads(dot_tn(ds, keys))
        yield
        for which, (ref, ext, part) in enumerate(((dk_buf, dke_ref, dk), (dv_buf, dve_ref, dv))):
            first = part[:edge]
            if i > 0:
                first = first + held[(i - 1, which)]
                ref[k0 : k0 + edge, cols] = first.astype(bf16)
            else:
                ext[:edge, cols] = first.astype(bf16)
            ref[k0 + edge : k0 + gk, cols] = part[edge:gk].astype(bf16)
            if i < n_ex - 2:
                held[(i, which)] = part[gk:]
            else:
                ext[edge:, cols] = part[gk:].astype(bf16)
        first = dq[:gq]
        if i > 0:
            dq_buf[q0 : q0 + gq, cols] = (first + held[(i - 1, 2)]).astype(bf16)
        else:
            dqe_ref[:gq, cols] = first.astype(bf16)
        if i < n_ex - 2:
            held[(i, 2)] = dq[gq:]
        else:
            dqe_ref[gq:, cols] = dq[gq:].astype(bf16)
        yield

    def copies(at):
        cols = pl.ds(pl.multiple_of(at * (BATCH * LANES), LANES), BATCH * LANES)
        out = []
        k_rows, q_rows = pl.ds(edge, (n_ex - 1) * gk - edge), pl.ds(gq, (n_ex - 2) * gq)
        for j, (buf, ref, rows) in enumerate(((dk_buf, dk_out, k_rows), (dv_buf, dv_out, k_rows), (dq_buf, dq_out, q_rows))):
            out.append(pltpu.make_async_copy(buf.at[rows, cols], ref.at[rows, cols], sems.at[at, j]))
        return out

    @pl.loop(0, q_ref.shape[1] // LANES // BATCH)
    def _(at):
        units = []
        for c in range(BATCH):
            cols = pl.ds(pl.multiple_of(at * (BATCH * LANES) + c * LANES, LANES), LANES)
            held = {}
            units += [unit(i, cols, held) for i in range(n_ex - 1)]
        run_skewed(units)
        for copy in copies(at):
            copy.start()

    @pl.loop(0, q_ref.shape[1] // LANES // BATCH)
    def _(at):
        for copy in copies(at):
            copy.wait()


def three_parts(x):
    hi = x.astype(jnp.bfloat16).astype(jnp.float32)
    mid = (x - hi).astype(jnp.bfloat16).astype(jnp.float32)
    return [hi, mid, x - hi - mid]


def stats_kernel(shape, pos_ref, dec_hbm, enc_hbm, q_hbm, o_hbm, g_hbm, k_hbm, me_ref, mo_ref, stat_ref, q_ref, o_ref, g_ref, k_ref, pack_ref, dec_ref, enc_ref, sems):
    bounds = Bounds(shape, (dec_ref, enc_ref, pos_ref))
    n_ex, gq, gk = bounds.n_ex, bounds.gq, bounds.gk
    edge = gk // 2
    last = (n_ex - 1) * gq
    feats = q_ref.shape[1]
    at_e = pl.multiple_of(jnp.where(bounds.even, last, 0), gq)
    at_o = pl.multiple_of(jnp.where(bounds.even, 0, last), gq)

    jobs = [
        (dec_hbm, dec_ref, None, None), (enc_hbm, enc_ref, None, None),
        (k_hbm, k_ref, (n_ex - 1) * gk, (0, gk)), (k_hbm, k_ref, 0, (gk, edge)),
    ]
    for src, dst in ((q_hbm, q_ref), (g_hbm, g_ref), (o_hbm, o_ref)):
        jobs += [(src, dst, last, (last, gq)), (src, dst, 0, (0, gq))]
    first = len(jobs)
    jobs += [(q_hbm, me_ref, at_e, (0, gq)), (g_hbm, me_ref, at_e, (gq, gq)), (q_hbm, mo_ref, at_o, (0, gq)), (g_hbm, mo_ref, at_o, (gq, gq))]
    jobs += [(src, dst, gq, (gq, last - gq)) for src, dst in ((q_hbm, q_ref), (g_hbm, g_ref), (o_hbm, o_ref))]
    copies = []
    for i, (src, dst, at, to) in enumerate(jobs):
        if to is not None:
            src, dst = src.at[pl.ds(at, to[1])], dst.at[pl.ds(*to), pl.ds(0, feats)]
        copies.append(pltpu.make_async_copy(src, dst, sems.at[i]))
    for copy in copies:
        copy.start()
    for copy in copies[:6]:
        copy.wait()

    slots = PER * gq
    per = 2 * gq * LANES // feats

    def keep(group, side, kind, value):
        stat_ref[2 * side + kind : 2 * side + kind + 1, group.lanes(slots)] = value
        for i, part in enumerate(three_parts(value)):
            pack_ref[side, group.row(per, 3 * kind + i), :] = part

    def log_unit(group):
        s = []
        for side in (0, 1):
            keys = k_ref[bounds.part(side), group.cols]
            s.append(dot_nt(keys, spread(bounds.own_rows(side, q_ref, group.cols))))
        yield
        for side in (0, 1):
            top, _, total = exp_top(bounds.edge_mask(side, s[side]))
            keep(group, side, 0, top + jnp.log(total))
        yield

    def dot_unit(group):
        for side in (0, 1):
            gs = spread(bounds.own_rows(side, g_ref, group.cols))
            keep(group, side, 1, row_dots(bounds.own_rows(side, o_ref, group.cols), gs))
        yield

    groups = feats // LANES
    each_group(groups, groups, lambda group: [log_unit(group)])
    for copy in copies[6:first]:
        copy.wait()
    each_group(groups, groups, lambda group: [dot_unit(group)])
    for copy in copies[first:]:
        copy.wait()
    after, before = pack_ref[0].astype(jnp.bfloat16), pack_ref[1].astype(jnp.bfloat16)
    me_ref[:, feats:] = jnp.where(bounds.even, after, before)
    mo_ref[:, feats:] = jnp.where(bounds.even, before, after)


def unpack(ref, group, per, i):
    return ref[group.row(per, i), :] + ref[group.row(per, i + 1), :] + ref[group.row(per, i + 2), :]


def remote_kernel(shape, *refs):
    *table, _, re_ref, ro_ref, k_ref, v_ref, me_ref, mo_ref, p_ref, ds_ref, got_ref, pack_ref = refs
    bounds = Bounds(shape, table)
    gq, gk = bounds.gq, bounds.gk
    even = bounds.even
    feats = k_ref.shape[1]
    slots = PER * gq
    slot = slot_of(gq)
    bf16, f32 = jnp.bfloat16, jnp.float32
    per_in, per_out = 2 * gq * LANES // feats, gq * LANES // feats
    extra = (slice(None), slice(feats, None))
    for side in (0, 1):
        got_ref[side] = bounds.from_side(side, re_ref, ro_ref, extra).astype(f32)
    pack_ref[...] = jnp.zeros_like(pack_ref)

    def unit(group):
        cols = group.cols
        work = []
        for side in (0, 1):
            far = bounds.from_side(side, re_ref, ro_ref, (slice(None), cols))
            keys = bounds.edge_rows(side, k_ref, cols)
            s = dot_nt(keys, spread(far[:gq]))
            dp = dot_nt(bounds.edge_rows(side, v_ref, cols), spread(far[gq:]))
            work.append((keys, s, dp))
        yield
        tops = [exp_top(bounds.edge_mask(side, work[side][1])) for side in (0, 1)]
        yield
        ds = []
        for side in (0, 1):
            top, e, total = tops[side]
            mine = top + jnp.log(total)
            whole = log_add(mine, unpack(got_ref.at[side], group, per_in, 0))
            dots = unpack(got_ref.at[side], group, per_in, 3)
            p = e * jnp.where(bounds.far_lanes(side, slot), jnp.exp(top - whole), 0.0)
            ds.append((p * (work[side][2] - dots)).astype(bf16))
            p_ref[bounds.part(side), group.lanes(slots)] = p.astype(bf16)
            ds_ref[bounds.part(side), group.lanes(slots)] = ds[side]
            for i, part in enumerate(three_parts(mine)):
                pack_ref[side, group.row(per_out, i), :] = part
        yield
        after, before = (gather_heads(dot_tn(ds[side], work[side][0])).astype(bf16) for side in (0, 1))
        yield
        me_ref[:, cols] = jnp.where(even, after, before)
        mo_ref[:, cols] = jnp.where(even, before, after)
        yield

    each_group(feats // LANES, feats // LANES, lambda group: [unit(group)])
    after, before = pack_ref[0].astype(bf16), pack_ref[1].astype(bf16)
    me_ref[:, feats:] = jnp.where(even, after, before)
    mo_ref[:, feats:] = jnp.where(even, before, after)


def ready_kernel(shape, *refs):
    *table, re_ref, ro_ref, own_ref, q_ref, g_ref, k_ref, v_ref, p_far, ds_far, dke_ref, dve_ref, p_ref, ds_ref, dk_ref, dv_ref = refs
    bounds = Bounds(shape, table)
    gq, gk = bounds.gq, bounds.gk
    edge = gk // 2
    slots = PER * gq
    slot = slot_of(gq)
    f32 = jnp.float32

    def far_unit(group):
        cols, lanes = group.cols, group.lanes(slots)
        far = [bounds.from_side(side, re_ref, ro_ref, (slice(None), cols)) for side in (0, 1)]
        for ref, ext, src, rows in ((dv_ref, dve_ref, p_far, slice(gq, None)), (dk_ref, dke_ref, ds_far, slice(0, gq))):
            a, b = (dot_nn(src[bounds.part(side), lanes], spread(far[side][rows])) for side in (0, 1))
            yield
            ref[:edge, cols] = a[:edge] + ext[edge:, cols].astype(f32)
            ref[edge:gk, cols] = a[edge:]
            ref[gk:, cols] = b + ext[:edge, cols].astype(f32)
        yield

    def own_unit(group):
        cols, lanes = group.cols, group.lanes(slots)
        work = []
        for side in (0, 1):
            s = dot_nt(bounds.edge_rows(side, k_ref, cols), spread(bounds.own_rows(side, q_ref, cols)))
            dp = dot_nt(bounds.edge_rows(side, v_ref, cols), spread(bounds.own_rows(side, g_ref, cols)))
            work.append((s, dp))
        yield
        for side in (0, 1):
            s, dp = work[side]
            logs = jnp.where(bounds.own_lanes(side, slot), own_ref[2 * side : 2 * side + 1, lanes], high)
            p = jnp.exp(bounds.edge_mask(side, s) - logs)
            p_ref[bounds.part(side), lanes] = p
            ds_ref[bounds.part(side), lanes] = p * (dp - own_ref[2 * side + 1 : 2 * side + 2, lanes])
        yield

    each_group(q_ref.shape[1] // LANES, 4, lambda group: [own_unit(group), far_unit(group)])


def edge_kernel(shape, *refs):
    *table, me_ref, mo_ref, own_ref, q_ref, g_ref, k_ref, p_ref, ds_ref, dka_ref, dva_ref, dqe_ref = refs[:14]
    _, _, _, dq_out, dk_out, dv_out, dq_buf, dk_buf, dv_buf, got_ref, sems = refs[14:]
    bounds = Bounds(shape, table)
    n_ex, gq, gk = bounds.n_ex, bounds.gq, bounds.gk
    edge = gk // 2
    feats = q_ref.shape[1]
    slots = PER * gq
    slot = slot_of(gq)
    bf16, f32 = jnp.bfloat16, jnp.float32
    last_q, last_k = (n_ex - 1) * gq, (n_ex - 1) * gk
    per = gq * LANES // feats
    extra = (slice(None), slice(feats, None))
    for side in (0, 1):
        got_ref[side] = bounds.from_side(side, me_ref, mo_ref, extra).astype(f32)

    def unit(group):
        cols, lanes = group.cols, group.lanes(slots)
        shares = []
        for side in (0, 1):
            other = unpack(got_ref.at[side], group, per, 0)
            if side == 0:
                other = jnp.where(bounds.has_next, other, low)
            own = own_ref[2 * side : 2 * side + 1, lanes]
            share = jnp.where(bounds.own_lanes(side, slot), jnp.exp(own - log_add(own, other)), 0.0)
            shares.append(share)
            part = bounds.part(side)
            dv = dot_nn((p_ref[part, lanes] * share).astype(bf16), spread(bounds.own_rows(side, g_ref, cols)))
            dv_buf[part, cols] = (dv + dva_ref[part, cols]).astype(bf16)
        yield
        ds = []
        for side in (0, 1):
            part = bounds.part(side)
            ds.append((ds_ref[part, lanes] * shares[side]).astype(bf16))
            dk = dot_nn(ds[side], spread(bounds.own_rows(side, q_ref, cols)))
            dk_buf[part, cols] = (dk + dka_ref[part, cols]).astype(bf16)
        yield
        for side in (0, 1):
            dq = gather_heads(dot_tn(ds[side], bounds.edge_rows(side, k_ref, cols)))
            back = bounds.from_side(side, me_ref, mo_ref, (slice(None), cols)).astype(f32)
            rows = slice(gq, 2 * gq) if side == 0 else slice(0, gq)
            dq_buf[rows, cols] = (dq + back + dqe_ref[rows, cols].astype(f32)).astype(bf16)
        if (group.c + 1) % CHUNK == 0:
            for copy in copies(group.c // CHUNK):
                copy.start()
        yield

    def copies(at):
        cols = pl.ds(at * (CHUNK * LANES), CHUNK * LANES)
        moves = []
        for buf, ref in ((dk_buf, dk_out), (dv_buf, dv_out)):
            moves += [(buf, (0, gk), ref, (last_k, gk)), (buf, (gk, edge), ref, (0, edge))]
        moves += [(dq_buf, (0, gq), dq_out, (0, gq)), (dq_buf, (gq, gq), dq_out, (last_q, gq))]
        return [
            pltpu.make_async_copy(src.at[pl.ds(*a), cols], dst.at[pl.ds(*b), cols], sems.at[at, j])
            for j, (src, a, dst, b) in enumerate(moves)
        ]

    each_group(feats // LANES, feats // LANES, lambda group: [unit(group)])
    for at in range(feats // LANES // CHUNK):
        for copy in copies(at):
            copy.wait()


inside = pl.BlockSpec(memory_space=pltpu.VMEM)
anywhere = pl.BlockSpec(memory_space=pl.ANY)
off_chip = pl.BlockSpec(memory_space=pltpu.HBM)
scalars = pl.BlockSpec(memory_space=pltpu.SMEM)


def call(kernel, ins, outs, scratch=(), aliases=None, flops=0, nbytes=0):
    return pl.pallas_call(
        kernel,
        out_shape=[shape for _, shape in outs],
        in_specs=list(ins),
        out_specs=[spec for spec, _ in outs],
        scratch_shapes=list(scratch),
        input_output_aliases=aliases or {},
        compiler_params=pltpu.CompilerParams(vmem_limit_bytes=40 * 1024 * 1024),
        cost_estimate=pl.CostEstimate(flops=flops, bytes_accessed=nbytes, transcendentals=0),
    )


def shards(dec_query, enc_key, enc_value, saved_out, d_out, dec_start, enc_start):
    q, k, v, o, g = dec_query[0], enc_key[0], enc_value[0], saved_out[0], d_out[0]
    q_rows, feats = q.shape
    k_rows = k.shape[0]
    pos = lax.axis_index("seq")
    count = lax.axis_size("seq")
    n_ex = (dec_start.shape[1] - 1) // count
    gq, gk = q_rows // n_ex, k_rows // n_ex
    edge = gk // 2
    groups = feats // LANES
    bf16, f32 = jnp.bfloat16, jnp.float32
    shape = (n_ex, gq, gk, count)

    def swap_even(x):
        return lax.ppermute(x, "seq", [(i, i ^ 1) for i in range(count) if i ^ 1 < count])

    def swap_odd(x):
        pairs = []
        for i in range(1, count - 1, 2):
            pairs += [(i, i + 1), (i + 1, i)]
        return lax.ppermute(x, "seq", pairs)

    place = pos.astype(jnp.int32)[None]
    table = (dec_start, enc_start, place)
    tables = [scalars] * 3

    packed = groups * PER * gq

    def like(rows, kind=bf16, width=feats):
        return jax.ShapeDtypeStruct((rows, width), kind)

    def vmem(rows):
        return pltpu.VMEM((rows, feats), bf16)

    def out(rows, kind=bf16, width=feats):
        return (inside, like(rows, kind, width))

    def pack(rows):
        return pltpu.VMEM((2, rows, PER * gq), f32)

    placed = (pltpu.with_memory_space_constraint(x, pltpu.HBM) for x in (dec_start, enc_start, q, o, g, k))
    raw_e, raw_o, own, q, o, g = call(
        functools.partial(stats_kernel, shape), [scalars] + [off_chip] * 6,
        [out(2 * gq, bf16, feats + PER * gq)] * 2 + [out(4, f32, packed)] + [out(q_rows)] * 3,
        scratch=[vmem(gk + edge), pack(2 * gq), pltpu.SMEM(dec_start.shape, jnp.int32), pltpu.SMEM(enc_start.shape, jnp.int32), pltpu.SemaphoreType.DMA((17,))],
        flops=int(4e8), nbytes=int(2e6),
    )(place, *placed)
    raw_e, raw_o = swap_even(raw_e), swap_odd(raw_o)

    big = [(anywhere, like(q_rows)), (anywhere, like(k_rows)), (anywhere, like(k_rows))]
    dq, dk, dv, dqe, dke, dve = call(
        functools.partial(interior_kernel, shape), tables + [anywhere] + [inside] * 5,
        big + [out(2 * gq), out(gk), out(gk)],
        scratch=[vmem(q_rows), vmem(k_rows), vmem(k_rows), pltpu.SemaphoreType.DMA((groups // BATCH, 3))],
        flops=int(4e9), nbytes=int(8e6),
    )(*table, own, q, o, g, k, v)

    to_e, to_o, p_far, ds_far = call(
        functools.partial(remote_kernel, shape), tables + [anywhere] + [inside] * 4,
        [out(gq, bf16, feats + PER * gq)] * 2 + [out(gk + edge, bf16, packed)] * 2,
        scratch=[pack(2 * gq), pack(gq)],
        flops=int(8e8), nbytes=int(3e6),
    )(*table, dqe, raw_e, raw_o, k, v)
    back_e, back_o = swap_even(to_e), swap_odd(to_o)

    p_own, ds_own, dka, dva = call(
        functools.partial(ready_kernel, shape), tables + [inside] * 11, [out(gk + edge, f32, packed)] * 2 + [out(gk + edge, f32)] * 2,
        flops=int(1e9), nbytes=int(6e6),
    )(*table, raw_e, raw_o, own, q, g, k, v, p_far, ds_far, dke, dve)
    dq, dk, dv = call(
        functools.partial(edge_kernel, shape), tables + [inside] * 11 + [anywhere] * 3, big,
        scratch=[vmem(2 * gq), vmem(gk + edge), vmem(gk + edge), pack(gq), pltpu.SemaphoreType.DMA((groups // CHUNK, 6))],
        aliases={14: 0, 15: 1, 16: 2},
        flops=int(1e9), nbytes=int(6e6),
    )(*table, back_e, back_o, own, q, g, k, p_own, ds_own, dka, dva, dqe, dq, dk, dv)
    return dq[None], dk[None], dv[None]


def solution(mesh):
    spec = P(("grp", "dp"), "seq", None)
    return jax.shard_map(
        shards,
        mesh=mesh,
        in_specs=(spec,) * 5 + (P(("grp", "dp"), None),) * 2,
        out_specs=(spec,) * 3,
        check_vma=False,
    )
```

```python
import functools

import jax
import jax.numpy as jnp
from jax import lax
from jax.experimental import pallas as pl
from jax.experimental.pallas import tpu as pltpu
from jax.sharding import PartitionSpec as P

H = 32
HD = 64
LANES = 256
PER = LANES // HD

low = -1e30
high = 1e30
BATCH = 4
CHUNK = 2


def dot_nt(a, b):
    return lax.dot_general(a, b, (((1,), (1,)), ((), ())), preferred_element_type=jnp.float32)


def dot_nn(a, b):
    return lax.dot_general(a, b, (((1,), (0,)), ((), ())), preferred_element_type=jnp.float32)


def dot_tn(a, b):
    return lax.dot_general(a, b, (((0,), (0,)), ((), ())), preferred_element_type=jnp.float32)


def spread(rows):
    half = LANES // 2
    side = lax.broadcasted_iota(jnp.int32, (rows.shape[0], half), 1) // HD
    empty = jnp.zeros((rows.shape[0], half), rows.dtype)
    out = []
    for h in range(PER):
        at, within = divmod(h * HD, half)
        piece = jnp.where(side == within // HD, rows[:, at * half : (at + 1) * half], empty)
        out.append(jnp.concatenate([piece if at == x else empty for x in range(LANES // half)], axis=1))
    return jnp.concatenate(out, axis=0)


def gather_heads(full):
    slots, half = full.shape[0] // PER, LANES // 2
    side = lax.broadcasted_iota(jnp.int32, (slots, half), 1) // HD
    out = []
    for at in range(LANES // half):
        lanes = slice(at * half, (at + 1) * half)
        heads = [h for h in range(PER) if h * HD // half == at]
        part = full[heads[0] * slots : (heads[0] + 1) * slots, lanes]
        for n, h in enumerate(heads[1:], 1):
            part = jnp.where(side == n, full[h * slots : (h + 1) * slots, lanes], part)
        out.append(part)
    return jnp.concatenate(out, axis=1)


def slot_of(slots):
    return lax.rem(lax.broadcasted_iota(jnp.int32, (1, PER * slots), 1), slots)


def row_dots(outs, spread_grads):
    slots = outs.shape[0]
    full = dot_nt(outs, spread_grads)
    row = lax.broadcasted_iota(jnp.int32, full.shape, 0)
    lane = lax.rem(lax.broadcasted_iota(jnp.int32, full.shape, 1), slots)
    return jnp.sum(jnp.where(row == lane, full, 0.0), axis=0, keepdims=True)


def log_add(a, b):
    top = jnp.maximum(a, b)
    return top + jnp.log(jnp.exp(a - top) + jnp.exp(b - top))


def row_ids(rows, lanes):
    return lax.broadcasted_iota(jnp.int32, (rows, lanes), 0)


def run_skewed(units, rate=1):
    live, queue = [], list(units)
    while queue or live:
        live += queue[:rate]
        queue = queue[rate:]
        for unit in list(live):
            try:
                next(unit)
            except StopIteration:
                live.remove(unit)


def each_group(groups, batch, units_of, rate=1):
    @pl.loop(0, groups // batch)
    def _(at):
        units = []
        for c in range(batch):
            units += units_of(Group(at * batch, c))
        run_skewed(units, rate)


class Group:
    def __init__(self, base, c):
        self.base, self.c = base, c
        self.cols = self.lanes(LANES)

    def lanes(self, width):
        return pl.ds(pl.multiple_of(self.base * width + self.c * width, width), width)

    def row(self, per, i):
        return pl.ds(pl.multiple_of(self.base * per, per) + (self.c * per + i), 1)


class Bounds:
    def __init__(self, shape, table):
        self.n_ex, self.gq, self.gk, self.count = shape
        self.dec_ref, self.enc_ref, pos_ref = table
        self.pos = pos_ref[0]
        self.even = lax.rem(self.pos, 2) == 0
        self.has_next = self.pos < self.count - 1

    def dec(self, i):
        return self.dec_ref[0, self.pos * self.n_ex + i] - self.pos * (self.n_ex * self.gq)

    def enc(self, i):
        return self.enc_ref[0, self.pos * self.n_ex + i] - self.pos * (self.n_ex * self.gk)

    def prior(self):
        at = jnp.maximum(self.pos * self.n_ex - 1, 0)
        rows = self.dec_ref[0, at] - self.pos * (self.n_ex * self.gq) + self.gq
        return jnp.where(self.pos > 0, rows, self.gq)

    def far_lanes(self, side, slot):
        return slot < self.dec(self.n_ex) - self.n_ex * self.gq if side == 0 else slot >= self.prior()

    def own_lanes(self, side, slot):
        return slot >= self.dec(self.n_ex - 1) - (self.n_ex - 1) * self.gq if side == 0 else slot < self.dec(0)

    def edge_mask(self, side, s):
        edge = self.gk // 2
        row = row_ids(edge, s.shape[1])
        if side == 1:
            return jnp.where(row < self.enc(0), s, low)
        first = self.enc(self.n_ex - 1) - (self.n_ex - 1) * self.gk
        return jnp.concatenate([jnp.where(row >= first, s[:edge], low), s[edge:]], axis=0)

    def edge_rows(self, side, ref, cols):
        return ref[ref.shape[0] - self.gk :, cols] if side == 0 else ref[: self.gk // 2, cols]

    def own_rows(self, side, ref, cols):
        return ref[ref.shape[0] - self.gq :, cols] if side == 0 else ref[: self.gq, cols]

    def part(self, side):
        return slice(0, self.gk) if side == 0 else slice(self.gk, self.gk + self.gk // 2)

    def from_side(self, side, even_ref, odd_ref, at):
        e, o = even_ref[at], odd_ref[at]
        return jnp.where(self.even, e, o) if side == 0 else jnp.where(self.even, o, e)


def exp_sum(s0, s1, s2):
    top = jnp.max(jnp.maximum(jnp.maximum(s0, s1), s2), axis=0, keepdims=True)
    e0, e1, e2 = jnp.exp(s0 - top), jnp.exp(s1 - top), jnp.exp(s2 - top)
    return top, e0, e1, e2, jnp.sum(e0 + e1 + e2, axis=0, keepdims=True)


def exp_top(s):
    top = jnp.max(s, axis=0, keepdims=True)
    e = jnp.exp(s - top)
    return top, e, jnp.sum(e, axis=0, keepdims=True)


def interior_kernel(shape, *refs):
    table, (_, q_ref, o_ref, g_ref, k_ref, v_ref), refs = refs[:3], refs[3:9], refs[9:]
    dq_out, dk_out, dv_out, dqe_ref, dke_ref, dve_ref, dq_buf, dk_buf, dv_buf, sems = refs
    bounds = Bounds(shape, table)
    n_ex, gq, gk = bounds.n_ex, bounds.gq, bounds.gk
    slots = 2 * gq
    edge = gk // 2
    win = gk + edge
    slot = slot_of(slots)
    bf16 = jnp.bfloat16

    def unit(i, cols, held):
        q0, k0 = i * gq, i * gk
        d_lo, d_hi = bounds.dec(i) - q0, bounds.dec(i + 1) - q0
        e_lo, e_hi = bounds.enc(i) - k0, bounds.enc(i + 1) - k0 - gk
        keys = k_ref[k0 : k0 + win, cols]
        qs = spread(q_ref[q0 : q0 + slots, cols])
        s = dot_nt(keys, qs)
        gs = spread(g_ref[q0 : q0 + slots, cols])
        dots = row_dots(o_ref[q0 : q0 + slots, cols], gs)
        dp = dot_nt(v_ref[k0 : k0 + win, cols], gs)
        yield
        row = row_ids(edge, LANES)
        s0 = jnp.where(row >= e_lo, s[:edge], low)
        s2 = jnp.where(row < e_hi, s[gk:], low)
        _, e0, e1, e2, total = exp_sum(s0, s[edge:gk], s2)
        yield
        inv = jnp.where((slot >= d_lo) & (slot < d_hi), 1.0 / total, 0.0)
        p = jnp.concatenate([e0, e1, e2], axis=0) * inv
        p_low = p.astype(bf16)
        yield
        dv = dot_nn(p_low, gs)
        ds = (p * (dp - dots)).astype(bf16)
        yield
        dk = dot_nn(ds, qs)
        dq = gather_heads(dot_tn(ds, keys))
        yield
        for which, (ref, ext, part) in enumerate(((dk_buf, dke_ref, dk), (dv_buf, dve_ref, dv))):
            first = part[:edge]
            if i > 0:
                first = first + held[(i - 1, which)]
                ref[k0 : k0 + edge, cols] = first.astype(bf16)
            else:
                ext[:edge, cols] = first.astype(bf16)
            ref[k0 + edge : k0 + gk, cols] = part[edge:gk].astype(bf16)
            if i < n_ex - 2:
                held[(i, which)] = part[gk:]
            else:
                ext[edge:, cols] = part[gk:].astype(bf16)
        first = dq[:gq]
        if i > 0:
            dq_buf[q0 : q0 + gq, cols] = (first + held[(i - 1, 2)]).astype(bf16)
        else:
            dqe_ref[:gq, cols] = first.astype(bf16)
        if i < n_ex - 2:
            held[(i, 2)] = dq[gq:]
        else:
            dqe_ref[gq:, cols] = dq[gq:].astype(bf16)
        yield

    def copies(at):
        cols = pl.ds(pl.multiple_of(at * (BATCH * LANES), LANES), BATCH * LANES)
        out = []
        k_rows, q_rows = pl.ds(edge, (n_ex - 1) * gk - edge), pl.ds(gq, (n_ex - 2) * gq)
        for j, (buf, ref, rows) in enumerate(((dk_buf, dk_out, k_rows), (dv_buf, dv_out, k_rows), (dq_buf, dq_out, q_rows))):
            out.append(pltpu.make_async_copy(buf.at[rows, cols], ref.at[rows, cols], sems.at[at, j]))
        return out

    @pl.loop(0, q_ref.shape[1] // LANES // BATCH)
    def _(at):
        units = []
        for c in range(BATCH):
            cols = pl.ds(pl.multiple_of(at * (BATCH * LANES) + c * LANES, LANES), LANES)
            held = {}
            units += [unit(i, cols, held) for i in range(n_ex - 1)]
        run_skewed(units)
        for copy in copies(at):
            copy.start()

    @pl.loop(0, q_ref.shape[1] // LANES // BATCH)
    def _(at):
        for copy in copies(at):
            copy.wait()


def three_parts(x):
    hi = x.astype(jnp.bfloat16).astype(jnp.float32)
    mid = (x - hi).astype(jnp.bfloat16).astype(jnp.float32)
    return [hi, mid, x - hi - mid]


def stats_kernel(shape, pos_ref, dec_hbm, enc_hbm, q_hbm, o_hbm, g_hbm, k_hbm, me_ref, mo_ref, stat_ref, q_ref, o_ref, g_ref, k_ref, pack_ref, dec_ref, enc_ref, sems):
    bounds = Bounds(shape, (dec_ref, enc_ref, pos_ref))
    n_ex, gq, gk = bounds.n_ex, bounds.gq, bounds.gk
    edge = gk // 2
    last = (n_ex - 1) * gq
    feats = q_ref.shape[1]
    at_e = pl.multiple_of(jnp.where(bounds.even, last, 0), gq)
    at_o = pl.multiple_of(jnp.where(bounds.even, 0, last), gq)

    jobs = [
        (dec_hbm, dec_ref, None, None), (enc_hbm, enc_ref, None, None),
        (k_hbm, k_ref, (n_ex - 1) * gk, (0, gk)), (k_hbm, k_ref, 0, (gk, edge)),
    ]
    for src, dst in ((q_hbm, q_ref), (g_hbm, g_ref), (o_hbm, o_ref)):
        jobs += [(src, dst, last, (last, gq)), (src, dst, 0, (0, gq))]
    first = len(jobs)
    jobs += [(q_hbm, me_ref, at_e, (0, gq)), (g_hbm, me_ref, at_e, (gq, gq)), (q_hbm, mo_ref, at_o, (0, gq)), (g_hbm, mo_ref, at_o, (gq, gq))]
    jobs += [(src, dst, gq, (gq, last - gq)) for src, dst in ((q_hbm, q_ref), (g_hbm, g_ref), (o_hbm, o_ref))]
    copies = []
    for i, (src, dst, at, to) in enumerate(jobs):
        if to is not None:
            src, dst = src.at[pl.ds(at, to[1])], dst.at[pl.ds(*to), pl.ds(0, feats)]
        copies.append(pltpu.make_async_copy(src, dst, sems.at[i]))
    for copy in copies:
        copy.start()
    for copy in copies[:6]:
        copy.wait()

    slots = PER * gq
    per = 2 * gq * LANES // feats

    def keep(group, side, kind, value):
        stat_ref[2 * side + kind : 2 * side + kind + 1, group.lanes(slots)] = value
        for i, part in enumerate(three_parts(value)):
            pack_ref[side, group.row(per, 3 * kind + i), :] = part

    def log_unit(group):
        s = []
        for side in (0, 1):
            keys = k_ref[bounds.part(side), group.cols]
            s.append(dot_nt(keys, spread(bounds.own_rows(side, q_ref, group.cols))))
        yield
        for side in (0, 1):
            top, _, total = exp_top(bounds.edge_mask(side, s[side]))
            keep(group, side, 0, top + jnp.log(total))
        yield

    def dot_unit(group):
        for side in (0, 1):
            gs = spread(bounds.own_rows(side, g_ref, group.cols))
            keep(group, side, 1, row_dots(bounds.own_rows(side, o_ref, group.cols), gs))
        yield

    groups = feats // LANES
    each_group(groups, groups, lambda group: [log_unit(group)])
    for copy in copies[6:first]:
        copy.wait()
    each_group(groups, groups, lambda group: [dot_unit(group)])
    for copy in copies[first:]:
        copy.wait()
    after, before = pack_ref[0].astype(jnp.bfloat16), pack_ref[1].astype(jnp.bfloat16)
    me_ref[:, feats:] = jnp.where(bounds.even, after, before)
    mo_ref[:, feats:] = jnp.where(bounds.even, before, after)


def unpack(ref, group, per, i):
    return ref[group.row(per, i), :] + ref[group.row(per, i + 1), :] + ref[group.row(per, i + 2), :]


def remote_kernel(shape, *refs):
    *table, _, re_ref, ro_ref, k_ref, v_ref, me_ref, mo_ref, p_ref, ds_ref, got_ref, pack_ref = refs
    bounds = Bounds(shape, table)
    gq, gk = bounds.gq, bounds.gk
    even = bounds.even
    feats = k_ref.shape[1]
    slots = PER * gq
    slot = slot_of(gq)
    bf16, f32 = jnp.bfloat16, jnp.float32
    per_in, per_out = 2 * gq * LANES // feats, gq * LANES // feats
    extra = (slice(None), slice(feats, None))
    for side in (0, 1):
        got_ref[side] = bounds.from_side(side, re_ref, ro_ref, extra).astype(f32)
    pack_ref[...] = jnp.zeros_like(pack_ref)

    def unit(group):
        cols = group.cols
        work = []
        for side in (0, 1):
            far = bounds.from_side(side, re_ref, ro_ref, (slice(None), cols))
            keys = bounds.edge_rows(side, k_ref, cols)
            s = dot_nt(keys, spread(far[:gq]))
            dp = dot_nt(bounds.edge_rows(side, v_ref, cols), spread(far[gq:]))
            work.append((keys, s, dp))
        yield
        tops = [exp_top(bounds.edge_mask(side, work[side][1])) for side in (0, 1)]
        yield
        ds = []
        for side in (0, 1):
            top, e, total = tops[side]
            mine = top + jnp.log(total)
            whole = log_add(mine, unpack(got_ref.at[side], group, per_in, 0))
            dots = unpack(got_ref.at[side], group, per_in, 3)
            p = e * jnp.where(bounds.far_lanes(side, slot), jnp.exp(top - whole), 0.0)
            ds.append((p * (work[side][2] - dots)).astype(bf16))
            p_ref[bounds.part(side), group.lanes(slots)] = p.astype(bf16)
            ds_ref[bounds.part(side), group.lanes(slots)] = ds[side]
            for i, part in enumerate(three_parts(mine)):
                pack_ref[side, group.row(per_out, i), :] = part
        yield
        after, before = (gather_heads(dot_tn(ds[side], work[side][0])).astype(bf16) for side in (0, 1))
        yield
        me_ref[:, cols] = jnp.where(even, after, before)
        mo_ref[:, cols] = jnp.where(even, before, after)
        yield

    each_group(feats // LANES, feats // LANES, lambda group: [unit(group)], rate=4)
    after, before = pack_ref[0].astype(bf16), pack_ref[1].astype(bf16)
    me_ref[:, feats:] = jnp.where(even, after, before)
    mo_ref[:, feats:] = jnp.where(even, before, after)


def ready_kernel(shape, *refs):
    *table, re_ref, ro_ref, own_ref, q_ref, g_ref, k_ref, v_ref, p_far, ds_far, dke_ref, dve_ref, p_ref, ds_ref, dk_ref, dv_ref = refs
    bounds = Bounds(shape, table)
    gq, gk = bounds.gq, bounds.gk
    edge = gk // 2
    slots = PER * gq
    slot = slot_of(gq)
    f32 = jnp.float32

    def far_unit(group):
        cols, lanes = group.cols, group.lanes(slots)
        far = [bounds.from_side(side, re_ref, ro_ref, (slice(None), cols)) for side in (0, 1)]
        for ref, ext, src, rows in ((dv_ref, dve_ref, p_far, slice(gq, None)), (dk_ref, dke_ref, ds_far, slice(0, gq))):
            a, b = (dot_nn(src[bounds.part(side), lanes], spread(far[side][rows])) for side in (0, 1))
            yield
            ref[:edge, cols] = a[:edge] + ext[edge:, cols].astype(f32)
            ref[edge:gk, cols] = a[edge:]
            ref[gk:, cols] = b + ext[:edge, cols].astype(f32)
        yield

    def own_unit(group):
        cols, lanes = group.cols, group.lanes(slots)
        work = []
        for side in (0, 1):
            s = dot_nt(bounds.edge_rows(side, k_ref, cols), spread(bounds.own_rows(side, q_ref, cols)))
            dp = dot_nt(bounds.edge_rows(side, v_ref, cols), spread(bounds.own_rows(side, g_ref, cols)))
            work.append((s, dp))
        yield
        for side in (0, 1):
            s, dp = work[side]
            logs = jnp.where(bounds.own_lanes(side, slot), own_ref[2 * side : 2 * side + 1, lanes], high)
            p = jnp.exp(bounds.edge_mask(side, s) - logs)
            p_ref[bounds.part(side), lanes] = p
            ds_ref[bounds.part(side), lanes] = p * (dp - own_ref[2 * side + 1 : 2 * side + 2, lanes])
        yield

    each_group(q_ref.shape[1] // LANES, 4, lambda group: [own_unit(group), far_unit(group)])


def edge_kernel(shape, *refs):
    *table, me_ref, mo_ref, own_ref, q_ref, g_ref, k_ref, p_ref, ds_ref, dka_ref, dva_ref, dqe_ref = refs[:14]
    _, _, _, dq_out, dk_out, dv_out, dq_buf, dk_buf, dv_buf, got_ref, sems = refs[14:]
    bounds = Bounds(shape, table)
    n_ex, gq, gk = bounds.n_ex, bounds.gq, bounds.gk
    edge = gk // 2
    feats = q_ref.shape[1]
    slots = PER * gq
    slot = slot_of(gq)
    bf16, f32 = jnp.bfloat16, jnp.float32
    last_q, last_k = (n_ex - 1) * gq, (n_ex - 1) * gk
    per = gq * LANES // feats
    extra = (slice(None), slice(feats, None))
    for side in (0, 1):
        got_ref[side] = bounds.from_side(side, me_ref, mo_ref, extra).astype(f32)

    def unit(group):
        cols, lanes = group.cols, group.lanes(slots)
        shares = []
        for side in (0, 1):
            other = unpack(got_ref.at[side], group, per, 0)
            if side == 0:
                other = jnp.where(bounds.has_next, other, low)
            own = own_ref[2 * side : 2 * side + 1, lanes]
            share = jnp.where(bounds.own_lanes(side, slot), jnp.exp(own - log_add(own, other)), 0.0)
            shares.append(share)
            part = bounds.part(side)
            dv = dot_nn((p_ref[part, lanes] * share).astype(bf16), spread(bounds.own_rows(side, g_ref, cols)))
            dv_buf[part, cols] = (dv + dva_ref[part, cols]).astype(bf16)
        yield
        ds = []
        for side in (0, 1):
            part = bounds.part(side)
            ds.append((ds_ref[part, lanes] * shares[side]).astype(bf16))
            dk = dot_nn(ds[side], spread(bounds.own_rows(side, q_ref, cols)))
            dk_buf[part, cols] = (dk + dka_ref[part, cols]).astype(bf16)
        yield
        for side in (0, 1):
            dq = gather_heads(dot_tn(ds[side], bounds.edge_rows(side, k_ref, cols)))
            back = bounds.from_side(side, me_ref, mo_ref, (slice(None), cols)).astype(f32)
            rows = slice(gq, 2 * gq) if side == 0 else slice(0, gq)
            dq_buf[rows, cols] = (dq + back + dqe_ref[rows, cols].astype(f32)).astype(bf16)
        if (group.c + 1) % CHUNK == 0:
            for copy in copies(group.c // CHUNK):
                copy.start()
        yield

    def copies(at):
        cols = pl.ds(at * (CHUNK * LANES), CHUNK * LANES)
        moves = []
        for buf, ref in ((dk_buf, dk_out), (dv_buf, dv_out)):
            moves += [(buf, (0, gk), ref, (last_k, gk)), (buf, (gk, edge), ref, (0, edge))]
        moves += [(dq_buf, (0, gq), dq_out, (0, gq)), (dq_buf, (gq, gq), dq_out, (last_q, gq))]
        return [
            pltpu.make_async_copy(src.at[pl.ds(*a), cols], dst.at[pl.ds(*b), cols], sems.at[at, j])
            for j, (src, a, dst, b) in enumerate(moves)
        ]

    each_group(feats // LANES, feats // LANES, lambda group: [unit(group)])
    for at in range(feats // LANES // CHUNK):
        for copy in copies(at):
            copy.wait()


inside = pl.BlockSpec(memory_space=pltpu.VMEM)
anywhere = pl.BlockSpec(memory_space=pl.ANY)
off_chip = pl.BlockSpec(memory_space=pltpu.HBM)
scalars = pl.BlockSpec(memory_space=pltpu.SMEM)


def call(kernel, ins, outs, scratch=(), aliases=None, flops=0, nbytes=0):
    return pl.pallas_call(
        kernel,
        out_shape=[shape for _, shape in outs],
        in_specs=list(ins),
        out_specs=[spec for spec, _ in outs],
        scratch_shapes=list(scratch),
        input_output_aliases=aliases or {},
        compiler_params=pltpu.CompilerParams(vmem_limit_bytes=40 * 1024 * 1024),
        cost_estimate=pl.CostEstimate(flops=flops, bytes_accessed=nbytes, transcendentals=0),
    )


def shards(dec_query, enc_key, enc_value, saved_out, d_out, dec_start, enc_start):
    q, k, v, o, g = dec_query[0], enc_key[0], enc_value[0], saved_out[0], d_out[0]
    q_rows, feats = q.shape
    k_rows = k.shape[0]
    pos = lax.axis_index("seq")
    count = lax.axis_size("seq")
    n_ex = (dec_start.shape[1] - 1) // count
    gq, gk = q_rows // n_ex, k_rows // n_ex
    edge = gk // 2
    groups = feats // LANES
    bf16, f32 = jnp.bfloat16, jnp.float32
    shape = (n_ex, gq, gk, count)

    def swap_even(x):
        return lax.ppermute(x, "seq", [(i, i ^ 1) for i in range(count) if i ^ 1 < count])

    def swap_odd(x):
        pairs = []
        for i in range(1, count - 1, 2):
            pairs += [(i, i + 1), (i + 1, i)]
        return lax.ppermute(x, "seq", pairs)

    place = pos.astype(jnp.int32)[None]
    table = (dec_start, enc_start, place)
    tables = [scalars] * 3

    packed = groups * PER * gq

    def like(rows, kind=bf16, width=feats):
        return jax.ShapeDtypeStruct((rows, width), kind)

    def vmem(rows):
        return pltpu.VMEM((rows, feats), bf16)

    def out(rows, kind=bf16, width=feats):
        return (inside, like(rows, kind, width))

    def pack(rows):
        return pltpu.VMEM((2, rows, PER * gq), f32)

    placed = (pltpu.with_memory_space_constraint(x, pltpu.HBM) for x in (dec_start, enc_start, q, o, g, k))
    raw_e, raw_o, own, q, o, g = call(
        functools.partial(stats_kernel, shape), [scalars] + [off_chip] * 6,
        [out(2 * gq, bf16, feats + PER * gq)] * 2 + [out(4, f32, packed)] + [out(q_rows)] * 3,
        scratch=[vmem(gk + edge), pack(2 * gq), pltpu.SMEM(dec_start.shape, jnp.int32), pltpu.SMEM(enc_start.shape, jnp.int32), pltpu.SemaphoreType.DMA((17,))],
        flops=int(4e8), nbytes=int(2e6),
    )(place, *placed)
    raw_e, raw_o = swap_even(raw_e), swap_odd(raw_o)

    big = [(anywhere, like(q_rows)), (anywhere, like(k_rows)), (anywhere, like(k_rows))]
    dq, dk, dv, dqe, dke, dve = call(
        functools.partial(interior_kernel, shape), tables + [anywhere] + [inside] * 5,
        big + [out(2 * gq), out(gk), out(gk)],
        scratch=[vmem(q_rows), vmem(k_rows), vmem(k_rows), pltpu.SemaphoreType.DMA((groups // BATCH, 3))],
        flops=int(4e9), nbytes=int(8e6),
    )(*table, own, q, o, g, k, v)

    to_e, to_o, p_far, ds_far = call(
        functools.partial(remote_kernel, shape), tables + [anywhere] + [inside] * 4,
        [out(gq, bf16, feats + PER * gq)] * 2 + [out(gk + edge, bf16, packed)] * 2,
        scratch=[pack(2 * gq), pack(gq)],
        flops=int(8e8), nbytes=int(3e6),
    )(*table, dqe, raw_e, raw_o, k, v)
    back_e, back_o = swap_even(to_e), swap_odd(to_o)

    p_own, ds_own, dka, dva = call(
        functools.partial(ready_kernel, shape), tables + [inside] * 11, [out(gk + edge, f32, packed)] * 2 + [out(gk + edge, f32)] * 2,
        flops=int(1e9), nbytes=int(6e6),
    )(*table, raw_e, raw_o, own, q, g, k, v, p_far, ds_far, dke, dve)
    dq, dk, dv = call(
        functools.partial(edge_kernel, shape), tables + [inside] * 11 + [anywhere] * 3, big,
        scratch=[vmem(2 * gq), vmem(gk + edge), vmem(gk + edge), pack(gq), pltpu.SemaphoreType.DMA((groups // CHUNK, 6))],
        aliases={14: 0, 15: 1, 16: 2},
        flops=int(1e9), nbytes=int(6e6),
    )(*table, back_e, back_o, own, q, g, k, p_own, ds_own, dka, dva, dqe, dq, dk, dv)
    return dq[None], dk[None], dv[None]


def solution(mesh):
    spec = P(("grp", "dp"), "seq", None)
    return jax.shard_map(
        shards,
        mesh=mesh,
        in_specs=(spec,) * 5 + (P(("grp", "dp"), None),) * 2,
        out_specs=(spec,) * 3,
        check_vma=False,
    )
```

```python
import functools

import jax
import jax.numpy as jnp
from jax import lax
from jax.experimental import pallas as pl
from jax.experimental.pallas import tpu as pltpu
from jax.sharding import PartitionSpec as P

H = 32
HD = 64
LANES = 256
PER = LANES // HD

low = -1e30
high = 1e30
BATCH = 4
CHUNK = 2


def dot_nt(a, b):
    return lax.dot_general(a, b, (((1,), (1,)), ((), ())), preferred_element_type=jnp.float32)


def dot_nn(a, b):
    return lax.dot_general(a, b, (((1,), (0,)), ((), ())), preferred_element_type=jnp.float32)


def dot_tn(a, b):
    return lax.dot_general(a, b, (((0,), (0,)), ((), ())), preferred_element_type=jnp.float32)


def spread(rows):
    half = LANES // 2
    side = lax.broadcasted_iota(jnp.int32, (rows.shape[0], half), 1) // HD
    empty = jnp.zeros((rows.shape[0], half), rows.dtype)
    out = []
    for h in range(PER):
        at, within = divmod(h * HD, half)
        piece = jnp.where(side == within // HD, rows[:, at * half : (at + 1) * half], empty)
        out.append(jnp.concatenate([piece if at == x else empty for x in range(LANES // half)], axis=1))
    return jnp.concatenate(out, axis=0)


def gather_heads(full):
    slots, half = full.shape[0] // PER, LANES // 2
    side = lax.broadcasted_iota(jnp.int32, (slots, half), 1) // HD
    out = []
    for at in range(LANES // half):
        lanes = slice(at * half, (at + 1) * half)
        heads = [h for h in range(PER) if h * HD // half == at]
        part = full[heads[0] * slots : (heads[0] + 1) * slots, lanes]
        for n, h in enumerate(heads[1:], 1):
            part = jnp.where(side == n, full[h * slots : (h + 1) * slots, lanes], part)
        out.append(part)
    return jnp.concatenate(out, axis=1)


def slot_of(slots):
    return lax.rem(lax.broadcasted_iota(jnp.int32, (1, PER * slots), 1), slots)


def row_dots(outs, spread_grads):
    slots = outs.shape[0]
    full = dot_nt(outs, spread_grads)
    row = lax.broadcasted_iota(jnp.int32, full.shape, 0)
    lane = lax.rem(lax.broadcasted_iota(jnp.int32, full.shape, 1), slots)
    return jnp.sum(jnp.where(row == lane, full, 0.0), axis=0, keepdims=True)


def log_add(a, b):
    top = jnp.maximum(a, b)
    return top + jnp.log(jnp.exp(a - top) + jnp.exp(b - top))


def row_ids(rows, lanes):
    return lax.broadcasted_iota(jnp.int32, (rows, lanes), 0)


def run_skewed(units, rate=1):
    live, queue = [], list(units)
    while queue or live:
        live += queue[:rate]
        queue = queue[rate:]
        for unit in list(live):
            try:
                next(unit)
            except StopIteration:
                live.remove(unit)


def each_group(groups, batch, units_of, rate=1):
    @pl.loop(0, groups // batch)
    def _(at):
        units = []
        for c in range(batch):
            units += units_of(Group(at * batch, c))
        run_skewed(units, rate)


class Group:
    def __init__(self, base, c):
        self.base, self.c = base, c
        self.cols = self.lanes(LANES)

    def lanes(self, width):
        return pl.ds(pl.multiple_of(self.base * width + self.c * width, width), width)

    def row(self, per, i):
        return pl.ds(pl.multiple_of(self.base * per, per) + (self.c * per + i), 1)


class Bounds:
    def __init__(self, shape, table):
        self.n_ex, self.gq, self.gk, self.count = shape
        self.dec_ref, self.enc_ref, pos_ref = table
        self.pos = pos_ref[0]
        self.even = lax.rem(self.pos, 2) == 0
        self.has_next = self.pos < self.count - 1

    def dec(self, i):
        return self.dec_ref[0, self.pos * self.n_ex + i] - self.pos * (self.n_ex * self.gq)

    def enc(self, i):
        return self.enc_ref[0, self.pos * self.n_ex + i] - self.pos * (self.n_ex * self.gk)

    def prior(self):
        at = jnp.maximum(self.pos * self.n_ex - 1, 0)
        rows = self.dec_ref[0, at] - self.pos * (self.n_ex * self.gq) + self.gq
        return jnp.where(self.pos > 0, rows, self.gq)

    def far_lanes(self, side, slot):
        return slot < self.dec(self.n_ex) - self.n_ex * self.gq if side == 0 else slot >= self.prior()

    def own_lanes(self, side, slot):
        return slot >= self.dec(self.n_ex - 1) - (self.n_ex - 1) * self.gq if side == 0 else slot < self.dec(0)

    def edge_mask(self, side, s):
        edge = self.gk // 2
        row = row_ids(edge, s.shape[1])
        if side == 1:
            return jnp.where(row < self.enc(0), s, low)
        first = self.enc(self.n_ex - 1) - (self.n_ex - 1) * self.gk
        return jnp.concatenate([jnp.where(row >= first, s[:edge], low), s[edge:]], axis=0)

    def edge_rows(self, side, ref, cols):
        return ref[ref.shape[0] - self.gk :, cols] if side == 0 else ref[: self.gk // 2, cols]

    def own_rows(self, side, ref, cols):
        return ref[ref.shape[0] - self.gq :, cols] if side == 0 else ref[: self.gq, cols]

    def part(self, side):
        return slice(0, self.gk) if side == 0 else slice(self.gk, self.gk + self.gk // 2)

    def from_side(self, side, even_ref, odd_ref, at):
        e, o = even_ref[at], odd_ref[at]
        return jnp.where(self.even, e, o) if side == 0 else jnp.where(self.even, o, e)


def exp_sum(s0, s1, s2):
    top = jnp.max(jnp.maximum(jnp.maximum(s0, s1), s2), axis=0, keepdims=True)
    e0, e1, e2 = jnp.exp(s0 - top), jnp.exp(s1 - top), jnp.exp(s2 - top)
    return top, e0, e1, e2, jnp.sum(e0 + e1 + e2, axis=0, keepdims=True)


def exp_top(s):
    top = jnp.max(s, axis=0, keepdims=True)
    e = jnp.exp(s - top)
    return top, e, jnp.sum(e, axis=0, keepdims=True)


def interior_kernel(shape, *refs):
    table, (_, q_ref, o_ref, g_ref, k_ref, v_ref), refs = refs[:3], refs[3:9], refs[9:]
    dq_out, dk_out, dv_out, dqe_ref, dke_ref, dve_ref, dq_buf, dk_buf, dv_buf, sems = refs
    bounds = Bounds(shape, table)
    n_ex, gq, gk = bounds.n_ex, bounds.gq, bounds.gk
    slots = 2 * gq
    edge = gk // 2
    win = gk + edge
    slot = slot_of(slots)
    bf16 = jnp.bfloat16

    def unit(i, cols, held):
        q0, k0 = i * gq, i * gk
        d_lo, d_hi = bounds.dec(i) - q0, bounds.dec(i + 1) - q0
        e_lo, e_hi = bounds.enc(i) - k0, bounds.enc(i + 1) - k0 - gk
        keys = k_ref[k0 : k0 + win, cols]
        qs = spread(q_ref[q0 : q0 + slots, cols])
        s = dot_nt(keys, qs)
        gs = spread(g_ref[q0 : q0 + slots, cols])
        dots = row_dots(o_ref[q0 : q0 + slots, cols], gs)
        dp = dot_nt(v_ref[k0 : k0 + win, cols], gs)
        yield
        row = row_ids(edge, LANES)
        s0 = jnp.where(row >= e_lo, s[:edge], low)
        s2 = jnp.where(row < e_hi, s[gk:], low)
        _, e0, e1, e2, total = exp_sum(s0, s[edge:gk], s2)
        yield
        inv = jnp.where((slot >= d_lo) & (slot < d_hi), 1.0 / total, 0.0)
        p = jnp.concatenate([e0, e1, e2], axis=0) * inv
        p_low = p.astype(bf16)
        yield
        dv = dot_nn(p_low, gs)
        ds = (p * (dp - dots)).astype(bf16)
        yield
        dk = dot_nn(ds, qs)
        dq = gather_heads(dot_tn(ds, keys))
        yield
        for which, (ref, ext, part) in enumerate(((dk_buf, dke_ref, dk), (dv_buf, dve_ref, dv))):
            first = part[:edge]
            if i > 0:
                first = first + held[(i - 1, which)]
                ref[k0 : k0 + edge, cols] = first.astype(bf16)
            else:
                ext[:edge, cols] = first.astype(bf16)
            ref[k0 + edge : k0 + gk, cols] = part[edge:gk].astype(bf16)
            if i < n_ex - 2:
                held[(i, which)] = part[gk:]
            else:
                ext[edge:, cols] = part[gk:].astype(bf16)
        first = dq[:gq]
        if i > 0:
            dq_buf[q0 : q0 + gq, cols] = (first + held[(i - 1, 2)]).astype(bf16)
        else:
            dqe_ref[:gq, cols] = first.astype(bf16)
        if i < n_ex - 2:
            held[(i, 2)] = dq[gq:]
        else:
            dqe_ref[gq:, cols] = dq[gq:].astype(bf16)
        yield

    def copies(at):
        cols = pl.ds(pl.multiple_of(at * (BATCH * LANES), LANES), BATCH * LANES)
        out = []
        k_rows, q_rows = pl.ds(edge, (n_ex - 1) * gk - edge), pl.ds(gq, (n_ex - 2) * gq)
        for j, (buf, ref, rows) in enumerate(((dk_buf, dk_out, k_rows), (dv_buf, dv_out, k_rows), (dq_buf, dq_out, q_rows))):
            out.append(pltpu.make_async_copy(buf.at[rows, cols], ref.at[rows, cols], sems.at[at, j]))
        return out

    @pl.loop(0, q_ref.shape[1] // LANES // BATCH)
    def _(at):
        units = []
        for c in range(BATCH):
            cols = pl.ds(pl.multiple_of(at * (BATCH * LANES) + c * LANES, LANES), LANES)
            held = {}
            units += [unit(i, cols, held) for i in range(n_ex - 1)]
        run_skewed(units)
        for copy in copies(at):
            copy.start()

    @pl.loop(0, q_ref.shape[1] // LANES // BATCH)
    def _(at):
        for copy in copies(at):
            copy.wait()


def three_parts(x):
    hi = x.astype(jnp.bfloat16).astype(jnp.float32)
    mid = (x - hi).astype(jnp.bfloat16).astype(jnp.float32)
    return [hi, mid, x - hi - mid]


def stats_kernel(shape, pos_ref, dec_hbm, enc_hbm, q_hbm, o_hbm, g_hbm, k_hbm, me_ref, mo_ref, stat_ref, q_ref, o_ref, g_ref, k_ref, pack_ref, dec_ref, enc_ref, sems):
    bounds = Bounds(shape, (dec_ref, enc_ref, pos_ref))
    n_ex, gq, gk = bounds.n_ex, bounds.gq, bounds.gk
    edge = gk // 2
    last = (n_ex - 1) * gq
    feats = q_ref.shape[1]
    at_e = pl.multiple_of(jnp.where(bounds.even, last, 0), gq)
    at_o = pl.multiple_of(jnp.where(bounds.even, 0, last), gq)

    jobs = [
        (k_hbm, k_ref, (n_ex - 1) * gk, (0, gk)), (k_hbm, k_ref, 0, (gk, edge)),
        (dec_hbm, dec_ref, None, None), (enc_hbm, enc_ref, None, None),
    ]
    for src, dst in ((q_hbm, q_ref), (g_hbm, g_ref), (o_hbm, o_ref)):
        jobs += [(src, dst, last, (last, gq)), (src, dst, 0, (0, gq))]
    first = len(jobs)
    jobs += [(q_hbm, me_ref, at_e, (0, gq)), (g_hbm, me_ref, at_e, (gq, gq)), (q_hbm, mo_ref, at_o, (0, gq)), (g_hbm, mo_ref, at_o, (gq, gq))]
    jobs += [(src, dst, gq, (gq, last - gq)) for src, dst in ((q_hbm, q_ref), (g_hbm, g_ref), (o_hbm, o_ref))]
    copies = []
    for i, (src, dst, at, to) in enumerate(jobs):
        if to is not None:
            src, dst = src.at[pl.ds(at, to[1])], dst.at[pl.ds(*to), pl.ds(0, feats)]
        copies.append(pltpu.make_async_copy(src, dst, sems.at[i]))
    for copy in copies:
        copy.start()
    for copy in copies[:6]:
        copy.wait()

    slots = PER * gq
    per = 2 * gq * LANES // feats

    def keep(group, side, kind, value):
        stat_ref[2 * side + kind : 2 * side + kind + 1, group.lanes(slots)] = value
        for i, part in enumerate(three_parts(value)):
            pack_ref[side, group.row(per, 3 * kind + i), :] = part

    def log_unit(group):
        s = []
        for side in (0, 1):
            keys = k_ref[bounds.part(side), group.cols]
            s.append(dot_nt(keys, spread(bounds.own_rows(side, q_ref, group.cols))))
        yield
        for side in (0, 1):
            top, _, total = exp_top(bounds.edge_mask(side, s[side]))
            keep(group, side, 0, top + jnp.log(total))
        yield

    def dot_unit(group):
        for side in (0, 1):
            gs = spread(bounds.own_rows(side, g_ref, group.cols))
            keep(group, side, 1, row_dots(bounds.own_rows(side, o_ref, group.cols), gs))
        yield

    groups = feats // LANES
    each_group(groups, groups, lambda group: [log_unit(group)])
    for copy in copies[6:first]:
        copy.wait()
    each_group(groups, groups, lambda group: [dot_unit(group)])
    for copy in copies[first:]:
        copy.wait()
    after, before = pack_ref[0].astype(jnp.bfloat16), pack_ref[1].astype(jnp.bfloat16)
    me_ref[:, feats:] = jnp.where(bounds.even, after, before)
    mo_ref[:, feats:] = jnp.where(bounds.even, before, after)


def unpack(ref, group, per, i):
    return ref[group.row(per, i), :] + ref[group.row(per, i + 1), :] + ref[group.row(per, i + 2), :]


def remote_kernel(shape, *refs):
    *table, _, re_ref, ro_ref, k_ref, v_ref, me_ref, mo_ref, p_ref, ds_ref, got_ref, pack_ref = refs
    bounds = Bounds(shape, table)
    gq, gk = bounds.gq, bounds.gk
    even = bounds.even
    feats = k_ref.shape[1]
    slots = PER * gq
    slot = slot_of(gq)
    bf16, f32 = jnp.bfloat16, jnp.float32
    per_in, per_out = 2 * gq * LANES // feats, gq * LANES // feats
    extra = (slice(None), slice(feats, None))
    for side in (0, 1):
        got_ref[side] = bounds.from_side(side, re_ref, ro_ref, extra).astype(f32)
    pack_ref[...] = jnp.zeros_like(pack_ref)

    def unit(group):
        cols = group.cols
        work = []
        for side in (0, 1):
            far = bounds.from_side(side, re_ref, ro_ref, (slice(None), cols))
            keys = bounds.edge_rows(side, k_ref, cols)
            s = dot_nt(keys, spread(far[:gq]))
            dp = dot_nt(bounds.edge_rows(side, v_ref, cols), spread(far[gq:]))
            work.append((keys, s, dp))
        yield
        tops = [exp_top(bounds.edge_mask(side, work[side][1])) for side in (0, 1)]
        yield
        ds = []
        for side in (0, 1):
            top, e, total = tops[side]
            mine = top + jnp.log(total)
            whole = log_add(mine, unpack(got_ref.at[side], group, per_in, 0))
            dots = unpack(got_ref.at[side], group, per_in, 3)
            p = e * jnp.where(bounds.far_lanes(side, slot), jnp.exp(top - whole), 0.0)
            ds.append((p * (work[side][2] - dots)).astype(bf16))
            p_ref[bounds.part(side), group.lanes(slots)] = p.astype(bf16)
            ds_ref[bounds.part(side), group.lanes(slots)] = ds[side]
            for i, part in enumerate(three_parts(mine)):
                pack_ref[side, group.row(per_out, i), :] = part
        yield
        after, before = (gather_heads(dot_tn(ds[side], work[side][0])).astype(bf16) for side in (0, 1))
        yield
        me_ref[:, cols] = jnp.where(even, after, before)
        mo_ref[:, cols] = jnp.where(even, before, after)
        yield

    each_group(feats // LANES, feats // LANES, lambda group: [unit(group)], rate=8)
    after, before = pack_ref[0].astype(bf16), pack_ref[1].astype(bf16)
    me_ref[:, feats:] = jnp.where(even, after, before)
    mo_ref[:, feats:] = jnp.where(even, before, after)


def ready_kernel(shape, *refs):
    *table, re_ref, ro_ref, own_ref, q_ref, g_ref, k_ref, v_ref, p_far, ds_far, dke_ref, dve_ref, p_ref, ds_ref, dk_ref, dv_ref = refs
    bounds = Bounds(shape, table)
    gq, gk = bounds.gq, bounds.gk
    edge = gk // 2
    slots = PER * gq
    slot = slot_of(gq)
    f32 = jnp.float32

    def far_unit(group):
        cols, lanes = group.cols, group.lanes(slots)
        far = [bounds.from_side(side, re_ref, ro_ref, (slice(None), cols)) for side in (0, 1)]
        for ref, ext, src, rows in ((dv_ref, dve_ref, p_far, slice(gq, None)), (dk_ref, dke_ref, ds_far, slice(0, gq))):
            a, b = (dot_nn(src[bounds.part(side), lanes], spread(far[side][rows])) for side in (0, 1))
            yield
            ref[:edge, cols] = a[:edge] + ext[edge:, cols].astype(f32)
            ref[edge:gk, cols] = a[edge:]
            ref[gk:, cols] = b + ext[:edge, cols].astype(f32)
        yield

    def own_unit(group):
        cols, lanes = group.cols, group.lanes(slots)
        work = []
        for side in (0, 1):
            s = dot_nt(bounds.edge_rows(side, k_ref, cols), spread(bounds.own_rows(side, q_ref, cols)))
            dp = dot_nt(bounds.edge_rows(side, v_ref, cols), spread(bounds.own_rows(side, g_ref, cols)))
            work.append((s, dp))
        yield
        for side in (0, 1):
            s, dp = work[side]
            logs = jnp.where(bounds.own_lanes(side, slot), own_ref[2 * side : 2 * side + 1, lanes], high)
            p = jnp.exp(bounds.edge_mask(side, s) - logs)
            p_ref[bounds.part(side), lanes] = p
            ds_ref[bounds.part(side), lanes] = p * (dp - own_ref[2 * side + 1 : 2 * side + 2, lanes])
        yield

    each_group(q_ref.shape[1] // LANES, 4, lambda group: [own_unit(group), far_unit(group)])


def edge_kernel(shape, *refs):
    *table, me_ref, mo_ref, own_ref, q_ref, g_ref, k_ref, p_ref, ds_ref, dka_ref, dva_ref, dqe_ref = refs[:14]
    _, _, _, dq_out, dk_out, dv_out, dq_buf, dk_buf, dv_buf, got_ref, sems = refs[14:]
    bounds = Bounds(shape, table)
    n_ex, gq, gk = bounds.n_ex, bounds.gq, bounds.gk
    edge = gk // 2
    feats = q_ref.shape[1]
    slots = PER * gq
    slot = slot_of(gq)
    bf16, f32 = jnp.bfloat16, jnp.float32
    last_q, last_k = (n_ex - 1) * gq, (n_ex - 1) * gk
    per = gq * LANES // feats
    extra = (slice(None), slice(feats, None))
    for side in (0, 1):
        got_ref[side] = bounds.from_side(side, me_ref, mo_ref, extra).astype(f32)

    def unit(group):
        cols, lanes = group.cols, group.lanes(slots)
        shares = []
        for side in (0, 1):
            other = unpack(got_ref.at[side], group, per, 0)
            if side == 0:
                other = jnp.where(bounds.has_next, other, low)
            own = own_ref[2 * side : 2 * side + 1, lanes]
            share = jnp.where(bounds.own_lanes(side, slot), jnp.exp(own - log_add(own, other)), 0.0)
            shares.append(share)
            part = bounds.part(side)
            dv = dot_nn((p_ref[part, lanes] * share).astype(bf16), spread(bounds.own_rows(side, g_ref, cols)))
            dv_buf[part, cols] = (dv + dva_ref[part, cols]).astype(bf16)
        yield
        ds = []
        for side in (0, 1):
            part = bounds.part(side)
            ds.append((ds_ref[part, lanes] * shares[side]).astype(bf16))
            dk = dot_nn(ds[side], spread(bounds.own_rows(side, q_ref, cols)))
            dk_buf[part, cols] = (dk + dka_ref[part, cols]).astype(bf16)
        yield
        for side in (0, 1):
            dq = gather_heads(dot_tn(ds[side], bounds.edge_rows(side, k_ref, cols)))
            back = bounds.from_side(side, me_ref, mo_ref, (slice(None), cols)).astype(f32)
            rows = slice(gq, 2 * gq) if side == 0 else slice(0, gq)
            dq_buf[rows, cols] = (dq + back + dqe_ref[rows, cols].astype(f32)).astype(bf16)
        if (group.c + 1) % CHUNK == 0:
            for copy in copies(group.c // CHUNK):
                copy.start()
        yield

    def copies(at):
        cols = pl.ds(at * (CHUNK * LANES), CHUNK * LANES)
        moves = []
        for buf, ref in ((dk_buf, dk_out), (dv_buf, dv_out)):
            moves += [(buf, (0, gk), ref, (last_k, gk)), (buf, (gk, edge), ref, (0, edge))]
        moves += [(dq_buf, (0, gq), dq_out, (0, gq)), (dq_buf, (gq, gq), dq_out, (last_q, gq))]
        return [
            pltpu.make_async_copy(src.at[pl.ds(*a), cols], dst.at[pl.ds(*b), cols], sems.at[at, j])
            for j, (src, a, dst, b) in enumerate(moves)
        ]

    each_group(feats // LANES, feats // LANES, lambda group: [unit(group)])
    for at in range(feats // LANES // CHUNK):
        for copy in copies(at):
            copy.wait()


inside = pl.BlockSpec(memory_space=pltpu.VMEM)
anywhere = pl.BlockSpec(memory_space=pl.ANY)
off_chip = pl.BlockSpec(memory_space=pltpu.HBM)
scalars = pl.BlockSpec(memory_space=pltpu.SMEM)


def call(kernel, ins, outs, scratch=(), aliases=None, flops=0, nbytes=0):
    return pl.pallas_call(
        kernel,
        out_shape=[shape for _, shape in outs],
        in_specs=list(ins),
        out_specs=[spec for spec, _ in outs],
        scratch_shapes=list(scratch),
        input_output_aliases=aliases or {},
        compiler_params=pltpu.CompilerParams(vmem_limit_bytes=40 * 1024 * 1024),
        cost_estimate=pl.CostEstimate(flops=flops, bytes_accessed=nbytes, transcendentals=0),
    )


def shards(dec_query, enc_key, enc_value, saved_out, d_out, dec_start, enc_start):
    q, k, v, o, g = dec_query[0], enc_key[0], enc_value[0], saved_out[0], d_out[0]
    q_rows, feats = q.shape
    k_rows = k.shape[0]
    pos = lax.axis_index("seq")
    count = lax.axis_size("seq")
    n_ex = (dec_start.shape[1] - 1) // count
    gq, gk = q_rows // n_ex, k_rows // n_ex
    edge = gk // 2
    groups = feats // LANES
    bf16, f32 = jnp.bfloat16, jnp.float32
    shape = (n_ex, gq, gk, count)

    def swap_even(x):
        return lax.ppermute(x, "seq", [(i, i ^ 1) for i in range(count) if i ^ 1 < count])

    def swap_odd(x):
        pairs = []
        for i in range(1, count - 1, 2):
            pairs += [(i, i + 1), (i + 1, i)]
        return lax.ppermute(x, "seq", pairs)

    place = pos.astype(jnp.int32)[None]
    table = (dec_start, enc_start, place)
    tables = [scalars] * 3

    packed = groups * PER * gq

    def like(rows, kind=bf16, width=feats):
        return jax.ShapeDtypeStruct((rows, width), kind)

    def vmem(rows):
        return pltpu.VMEM((rows, feats), bf16)

    def out(rows, kind=bf16, width=feats):
        return (inside, like(rows, kind, width))

    def pack(rows):
        return pltpu.VMEM((2, rows, PER * gq), f32)

    placed = (pltpu.with_memory_space_constraint(x, pltpu.HBM) for x in (dec_start, enc_start, q, o, g, k))
    raw_e, raw_o, own, q, o, g = call(
        functools.partial(stats_kernel, shape), [scalars] + [off_chip] * 6,
        [out(2 * gq, bf16, feats + PER * gq)] * 2 + [out(4, f32, packed)] + [out(q_rows)] * 3,
        scratch=[vmem(gk + edge), pack(2 * gq), pltpu.SMEM(dec_start.shape, jnp.int32), pltpu.SMEM(enc_start.shape, jnp.int32), pltpu.SemaphoreType.DMA((17,))],
        flops=int(4e8), nbytes=int(2e6),
    )(place, *placed)
    raw_e, raw_o = swap_even(raw_e), swap_odd(raw_o)

    big = [(anywhere, like(q_rows)), (anywhere, like(k_rows)), (anywhere, like(k_rows))]
    dq, dk, dv, dqe, dke, dve = call(
        functools.partial(interior_kernel, shape), tables + [anywhere] + [inside] * 5,
        big + [out(2 * gq), out(gk), out(gk)],
        scratch=[vmem(q_rows), vmem(k_rows), vmem(k_rows), pltpu.SemaphoreType.DMA((groups // BATCH, 3))],
        flops=int(4e9), nbytes=int(8e6),
    )(*table, own, q, o, g, k, v)

    to_e, to_o, p_far, ds_far = call(
        functools.partial(remote_kernel, shape), tables + [anywhere] + [inside] * 4,
        [out(gq, bf16, feats + PER * gq)] * 2 + [out(gk + edge, bf16, packed)] * 2,
        scratch=[pack(2 * gq), pack(gq)],
        flops=int(8e8), nbytes=int(3e6),
    )(*table, dqe, raw_e, raw_o, k, v)
    back_e, back_o = swap_even(to_e), swap_odd(to_o)

    p_own, ds_own, dka, dva = call(
        functools.partial(ready_kernel, shape), tables + [inside] * 11, [out(gk + edge, f32, packed)] * 2 + [out(gk + edge, f32)] * 2,
        flops=int(1e9), nbytes=int(6e6),
    )(*table, raw_e, raw_o, own, q, g, k, v, p_far, ds_far, dke, dve)
    dq, dk, dv = call(
        functools.partial(edge_kernel, shape), tables + [inside] * 11 + [anywhere] * 3, big,
        scratch=[vmem(2 * gq), vmem(gk + edge), vmem(gk + edge), pack(gq), pltpu.SemaphoreType.DMA((groups // CHUNK, 6))],
        aliases={14: 0, 15: 1, 16: 2},
        flops=int(1e9), nbytes=int(6e6),
    )(*table, back_e, back_o, own, q, g, k, p_own, ds_own, dka, dva, dqe, dq, dk, dv)
    return dq[None], dk[None], dv[None]


def solution(mesh):
    spec = P(("grp", "dp"), "seq", None)
    return jax.shard_map(
        shards,
        mesh=mesh,
        in_specs=(spec,) * 5 + (P(("grp", "dp"), None),) * 2,
        out_specs=(spec,) * 3,
        check_vma=False,
    )
```
